32 devices in a mesh: wide: 16 (over z, x, core), narrow: 2 (over y).
Axes of the slice: x: 2, y: 2, z: 4, core: 2. Of those that a mesh axis runs over, the one named last changes fastest.
Arguments:
- tokens: bfloat16 [32, 16384], P('wide', 'narrow'), may hold values from -6 to 6
- q_weight: bfloat16 [16384, 16384], P('narrow', 'wide'), may hold values from -0.046875 to 0.046875
- key_value_weight: bfloat16 [16384, 2048], P('narrow', 'wide'), may hold values from -0.046875 to 0.046875
- out_weight: bfloat16 [16384, 16384], P('narrow', 'wide'), may hold values from -0.046875 to 0.046875
- stored_keys: bfloat16 [32, 256, 1024], P(('wide', 'narrow')), may hold values from -6 to 6
- stored_values: bfloat16 [32, 256, 1024], P(('wide', 'narrow')), may hold values from -6 to 6
- channel_key_scale: float32 [32, 1024], P(('wide', 'narrow')), may hold values from 0.5 to 64
- lengths: int32 [32], P(('wide', 'narrow')), may hold values from 1 to 256, 4096 in all
Outputs:
- attn_out: bfloat16 [32, 16384], P('narrow', 'wide')
The draws below stay inside these ranges and needn't reach their ends.
Inputs may be any that keep to these rules, and one draw needn't show every extreme that they name: `lengths`: each request holds 1 to 256 cached tokens, and some request holds exactly 256.
All inputs are finite; a program needn't handle non-finite values. No bound on the sum of `lengths` on one device may be relied on, other than what follows from the above.
Results may differ from the reference program's by a relative error of at most 0.005.
The reference program's roundings to bfloat16 on the way count: a program that leaves them out, or rounds other values in their place, can miss the bound.
Values may be sent and summed in bfloat16 or wider, within the bound.
No kernel may reach another device: no remote copies, remote signals or barrier semaphores. Data moves between devices by JAX's collectives and lax.ppermute only.
A program may use at most 128 MiB of HBM per device.

```python
import math
import jax
import jax.numpy as jnp
import numpy as np
from jax import lax

MODEL_WIDTH = 16384
QUERY_HEADS = 128
KEY_VALUE_HEADS = 8
HEAD_SIZE = 128
CACHE_SLOTS = 256
REQUEST_COUNT = 32


def draw_channel_key_scale(key, part):
    leading_key = jax.random.fold_in(jax.random.fold_in(key, 17), 0)
    channel_index = jnp.exp(jax.random.uniform(leading_key, (REQUEST_COUNT, KEY_VALUE_HEADS * HEAD_SIZE), jnp.float32, math.log(0.5), math.log(2.0)))
    return channel_index.astype(jnp.float32)


def shard_levels(stream_key, extent, shards, smallest, high):
    gain = 1.0
    for position, parts in shards:
        steps = jax.random.uniform(jax.random.fold_in(jax.random.fold_in(stream_key, 6), position), (parts,), jnp.float32, smallest / len(shards), high / len(shards))
        gain = gain * jnp.repeat(jnp.exp(steps), extent[position] // parts).reshape((-1,) + (1,) * (len(extent) - 1 - position))
    return gain


def split_up(amount, total, reach, lean):
    portions = [(1 << 20) // math.isqrt(standing ** lean) + 1 for standing in range(2, amount + 1)]
    rest, given = total - reach - (amount - 1), [1] * (amount - 1)
    while rest > 0:
        free = [i for i in range(amount - 1) if given[i] < reach]
        pool, budget = sum([portions[i] for i in free]), rest
        for i in free:
            more = min(reach - given[i], max(1, budget * portions[i] // pool), rest)
            given[i] = given[i] + more
            rest = rest - more
    return np.array([reach] + given)


def uneven(key, number_of, total, bound, skew):
    if number_of == 2:
        one = jax.random.randint(key, (), max(1, total - bound), min(bound, total - 1) + 1)
        return jnp.stack([one, total - one])
    sizes = jnp.asarray(split_up(number_of, total, bound, skew), jnp.int32)
    twos = (number_of - 1) // 2
    source_of, sink = sizes[1:1 + 2 * twos:2], sizes[2:2 + 2 * twos:2]
    room = jnp.minimum(source_of - 1, bound - sink)
    passed = jax.random.randint(jax.random.fold_in(key, 1), (twos,), 0, 1 << 20) % (room + 1)
    sizes = sizes.at[1:1 + 2 * twos:2].set(source_of - passed).at[2:2 + 2 * twos:2].set(sink + passed)
    return sizes[jax.random.permutation(jax.random.fold_in(key, 2), number_of)]


def normal_values(key, extent, scale, bound, shards=(), kind=jnp.bfloat16):
    drawn = jax.random.normal(key, extent, jnp.float32) * scale
    if len(shards) > 0:
        drawn = shard_levels(key, extent, shards, -0.22, 0.18) * drawn
    return jnp.clip(drawn, min=-bound, max=bound).astype(kind)


def setup_inputs(seed: int = 0) -> dict:
    keys = jax.random.split(jax.random.key(seed), 9)
    tokens = normal_values(keys[0], (REQUEST_COUNT, MODEL_WIDTH), 1.0, 6.0, ((0, 16), (1, 2)))
    q_weight = normal_values(keys[1], (MODEL_WIDTH, QUERY_HEADS * HEAD_SIZE), MODEL_WIDTH ** -0.5, 0.046875, ((0, 2), (1, 16)))
    key_value_weight = normal_values(keys[2], (MODEL_WIDTH, 2 * KEY_VALUE_HEADS * HEAD_SIZE), MODEL_WIDTH ** -0.5, 0.046875, ((0, 2), (1, 16)))
    out_weight = normal_values(keys[3], (QUERY_HEADS * HEAD_SIZE, MODEL_WIDTH), (QUERY_HEADS * HEAD_SIZE) ** -0.5, 0.046875, ((0, 2), (1, 16)))
    stored_keys = normal_values(keys[4], (REQUEST_COUNT, CACHE_SLOTS, KEY_VALUE_HEADS * HEAD_SIZE), 1.0, 6.0, ((0, 32),))
    stored_values = normal_values(keys[5], (REQUEST_COUNT, CACHE_SLOTS, KEY_VALUE_HEADS * HEAD_SIZE), 1.0, 6.0, ((0, 32),))
    channel_key_scale = draw_channel_key_scale(jax.random.fold_in(keys[8], 71), 0)
    lengths = uneven(keys[7], REQUEST_COUNT, REQUEST_COUNT * CACHE_SLOTS // 2, CACHE_SLOTS, 2).astype(jnp.int32)
    return dict(tokens=tokens, q_weight=q_weight, key_value_weight=key_value_weight, out_weight=out_weight, stored_keys=stored_keys, stored_values=stored_values, channel_key_scale=channel_key_scale, lengths=lengths)


def apply_rotation(values, token_position):
    half = values.shape[-1] // 2
    freq = jnp.exp(jnp.arange(half, dtype=jnp.float32) * (-2.0 * math.log(500000.0) / HEAD_SIZE))
    angle = token_position * freq
    cosine = jnp.cos(angle)
    sine = jnp.sin(angle)
    first = values[..., :half]
    second = values[..., half:]
    return jnp.concatenate([first * cosine - second * sine, second * cosine + first * sine], axis=-1)


def attend(query_vector, current_token, stored_keys, stored_values, channel_key_scale, lengths):
    owning_devices = query_vector.shape[0]
    slot_indices = stored_keys.shape[1]
    group_index = QUERY_HEADS // KEY_VALUE_HEADS
    inverse_scale = HEAD_SIZE ** -0.5
    token_position = lengths.astype(jnp.float32)
    rotated_query = apply_rotation(query_vector.astype(jnp.float32).reshape(owning_devices, KEY_VALUE_HEADS, group_index, HEAD_SIZE), token_position[:, None, None, None])
    rotated_key = apply_rotation(current_token[:, :KEY_VALUE_HEADS * HEAD_SIZE].astype(jnp.float32).reshape(owning_devices, KEY_VALUE_HEADS, HEAD_SIZE), token_position[:, None, None])
    current_value = current_token[:, KEY_VALUE_HEADS * HEAD_SIZE:].reshape(owning_devices, KEY_VALUE_HEADS, HEAD_SIZE)
    stored_query = (rotated_query * channel_key_scale.reshape(owning_devices, KEY_VALUE_HEADS, 1, HEAD_SIZE) * inverse_scale).astype(jnp.bfloat16)
    fresh_query = (rotated_query * inverse_scale).astype(jnp.bfloat16)
    fresh_key = rotated_key.astype(jnp.bfloat16)
    keys_divided = stored_keys.reshape(owning_devices, slot_indices, KEY_VALUE_HEADS, HEAD_SIZE)
    values_divided = stored_values.reshape(owning_devices, slot_indices, KEY_VALUE_HEADS, HEAD_SIZE)
    scores = jnp.einsum("rgic,rpgc->rgip", stored_query.astype(jnp.float32), keys_divided.astype(jnp.float32))
    fresh_score = jnp.sum(fresh_query.astype(jnp.float32) * fresh_key.astype(jnp.float32)[:, :, None, :], axis=-1)
    valid = jnp.arange(slot_indices, dtype=jnp.int32)[None, None, None, :] < lengths.astype(jnp.int32)[:, None, None, None]
    masked = jnp.where(valid, scores, jnp.float32(-1e30))
    top = jnp.maximum(jnp.max(masked, axis=-1), fresh_score)
    exps = jnp.where(valid, jnp.exp(masked - top[..., None]), jnp.float32(0.0))
    fresh_exp = jnp.exp(fresh_score - top)
    total = jnp.sum(exps, axis=-1) + fresh_exp
    weights = exps.astype(jnp.bfloat16)
    fresh_weight = fresh_exp.astype(jnp.bfloat16)
    summed = jnp.einsum("rgip,rpgc->rgic", weights.astype(jnp.float32), values_divided.astype(jnp.float32))
    summed = summed + fresh_weight.astype(jnp.float32)[..., None] * current_value.astype(jnp.float32)[:, :, None, :]
    return (summed / total[..., None]).astype(jnp.bfloat16).reshape(owning_devices, QUERY_HEADS * HEAD_SIZE)


def reference(tokens, q_weight, key_value_weight, out_weight, stored_keys, stored_values, channel_key_scale, lengths):
    query_vector = jnp.dot(tokens, q_weight, preferred_element_type=jnp.float32).astype(jnp.bfloat16)
    current_token = jnp.dot(tokens, key_value_weight, preferred_element_type=jnp.float32).astype(jnp.bfloat16)

    def one_request(items):
        expanded = [item[None] for item in items]
        return attend(*expanded)[0]

    attended = lax.map(one_request, (query_vector, current_token, stored_keys, stored_values, channel_key_scale, lengths))
    return jnp.dot(attended, out_weight, preferred_element_type=jnp.float32).astype(jnp.bfloat16)
```

```python
import math

import jax
import jax.numpy as jnp
from jax import lax
from jax.sharding import Mesh
from jax.sharding import PartitionSpec as P

QUERY_HEADS = 128
KEY_VALUE_HEADS = 8
HEAD_SIZE = 128

WIDE = ("hi", "lo")
EVERY = ("hi", "lo", "narrow")


def apply_rotation(values, token_position):
    half = values.shape[-1] // 2
    freq = jnp.exp(jnp.arange(half, dtype=jnp.float32) * (-2.0 * math.log(500000.0) / HEAD_SIZE))
    angle = token_position * freq
    cosine = jnp.cos(angle)
    sine = jnp.sin(angle)
    first = values[..., :half]
    second = values[..., half:]
    return jnp.concatenate(
        [first * cosine - second * sine, second * cosine + first * sine], axis=-1
    )


def attend(query_vector, current_token, stored_keys, stored_values, channel_key_scale, lengths):
    owning_devices = query_vector.shape[0]
    slot_indices = stored_keys.shape[1]
    group_index = QUERY_HEADS // KEY_VALUE_HEADS
    inverse_scale = HEAD_SIZE ** (-0.5)
    token_position = lengths.astype(jnp.float32)
    rotated_query = apply_rotation(
        query_vector.astype(jnp.float32).reshape(
            owning_devices, KEY_VALUE_HEADS, group_index, HEAD_SIZE
        ),
        token_position[:, None, None, None],
    )
    rotated_key = apply_rotation(
        current_token[:, : KEY_VALUE_HEADS * HEAD_SIZE]
        .astype(jnp.float32)
        .reshape(owning_devices, KEY_VALUE_HEADS, HEAD_SIZE),
        token_position[:, None, None],
    )
    current_value = current_token[:, KEY_VALUE_HEADS * HEAD_SIZE :].reshape(
        owning_devices, KEY_VALUE_HEADS, HEAD_SIZE
    )
    stored_query = (
        rotated_query
        * channel_key_scale.reshape(owning_devices, KEY_VALUE_HEADS, 1, HEAD_SIZE)
        * inverse_scale
    ).astype(jnp.bfloat16)
    fresh_query = (rotated_query * inverse_scale).astype(jnp.bfloat16)
    fresh_key = rotated_key.astype(jnp.bfloat16)
    keys_divided = stored_keys.reshape(owning_devices, slot_indices, KEY_VALUE_HEADS, HEAD_SIZE)
    values_divided = stored_values.reshape(owning_devices, slot_indices, KEY_VALUE_HEADS, HEAD_SIZE)
    scores = jnp.einsum(
        "rgic,rpgc->rgip", stored_query, keys_divided, preferred_element_type=jnp.float32
    )
    fresh_score = jnp.sum(
        fresh_query.astype(jnp.float32) * fresh_key.astype(jnp.float32)[:, :, None, :], axis=-1
    )
    valid = (
        jnp.arange(slot_indices, dtype=jnp.int32)[None, None, None, :]
        < lengths[:, None, None, None]
    )
    masked = jnp.where(valid, scores, jnp.float32(-1e30))
    top = jnp.maximum(jnp.max(masked, axis=-1), fresh_score)
    exps = jnp.where(valid, jnp.exp(masked - top[..., None]), jnp.float32(0.0))
    fresh_exp = jnp.exp(fresh_score - top)
    total = jnp.sum(exps, axis=-1) + fresh_exp
    weights = exps.astype(jnp.bfloat16)
    fresh_weight = fresh_exp.astype(jnp.bfloat16)
    summed = jnp.einsum(
        "rgip,rpgc->rgic", weights, values_divided, preferred_element_type=jnp.float32
    )
    summed = (
        summed
        + fresh_weight.astype(jnp.float32)[..., None]
        * current_value.astype(jnp.float32)[:, :, None, :]
    )
    return (
        (summed / total[..., None])
        .astype(jnp.bfloat16)
        .reshape(owning_devices, QUERY_HEADS * HEAD_SIZE)
    )


def gather_wide(block):
    count = lax.axis_size(WIDE)
    me = lax.axis_index(WIDE)
    held = block
    depth = 0
    step = count // 2
    while step:
        other = lax.ppermute(held, WIDE, [(i, i ^ step) for i in range(count)])
        upper = (me & step) != 0
        held = jnp.stack(
            [jnp.where(upper, other, held), jnp.where(upper, held, other)], axis=depth
        )
        depth += 1
        step //= 2
    return held.reshape((count * block.shape[0],) + block.shape[1:])


def body(
    tokens,
    q_weight,
    key_value_weight,
    out_weight,
    stored_keys,
    stored_values,
    channel_key_scale,
    lengths,
):
    high = lax.axis_size("hi")
    low = lax.axis_size("lo")
    wide_count = high * low
    narrow = lax.axis_size("narrow")
    query_cols = q_weight.shape[1]
    row_width = query_cols + key_value_weight.shape[1]
    per_owner = stored_keys.shape[0]
    piece = gather_wide(tokens)
    partial_terms = jnp.concatenate(
        [
            jnp.dot(piece, q_weight, preferred_element_type=jnp.float32),
            jnp.dot(piece, key_value_weight, preferred_element_type=jnp.float32),
        ],
        axis=1,
    )
    received = lax.all_to_all(partial_terms, EVERY, split_axis=0, concat_axis=0, tiled=True)
    received = received.reshape(wide_count, narrow, per_owner, row_width)
    owned = jnp.sum(received, axis=1).astype(jnp.bfloat16).transpose(1, 0, 2)
    query_vector = owned[:, :, :query_cols].reshape(per_owner, wide_count * query_cols)
    current_token = owned[:, :, query_cols:].reshape(
        per_owner, wide_count * (row_width - query_cols)
    )
    attended = attend(
        query_vector, current_token, stored_keys, stored_values, channel_key_scale, lengths
    )
    depth = out_weight.shape[0]
    parts = attended.reshape(per_owner, narrow, depth).transpose(1, 0, 2)
    parts = jnp.broadcast_to(parts[None], (high, narrow, per_owner, depth))
    mine = lax.all_to_all(
        parts.reshape(high * narrow * per_owner, depth),
        ("hi", "narrow"),
        split_axis=0,
        concat_axis=0,
        tiled=True,
    ).reshape(high, 1, narrow * per_owner, depth)
    ordered = lax.all_gather(mine, "lo", axis=1, tiled=True)
    ordered = ordered.reshape(wide_count * narrow * per_owner, depth)
    terms = jnp.dot(ordered, out_weight, preferred_element_type=jnp.float32)
    return sum_narrow(terms).astype(jnp.bfloat16)


def sum_narrow(terms):
    narrow = lax.axis_size("narrow")
    me = lax.axis_index("narrow")
    rows = terms.shape[0] // narrow
    grouped = terms.reshape(narrow, rows, terms.shape[1])
    total = lax.dynamic_index_in_dim(grouped, me, 0, keepdims=False)
    for step in range(1, narrow):
        target = lax.rem(me + step, narrow)
        leaving = lax.dynamic_index_in_dim(grouped, target, 0, keepdims=False)
        total = total + lax.ppermute(
            leaving, "narrow", [(i, (i + step) % narrow) for i in range(narrow)]
        )
    return total


def solution(mesh):
    high, low, narrow = mesh.shape["wide"] // 2, 2, mesh.shape["narrow"]
    fine = Mesh(mesh.devices.reshape(high, low, narrow), EVERY)
    placed = (
        P(WIDE, "narrow"),
        P("narrow", WIDE),
        P("narrow", WIDE),
        P("narrow", WIDE),
        P(EVERY, None, None),
        P(EVERY, None, None),
        P(EVERY, None),
        P(EVERY),
    )
    return jax.shard_map(
        body, mesh=fine, in_specs=placed, out_specs=P("narrow", WIDE), check_vma=False
    )
```

```python
import functools
import math

import jax
import jax.numpy as jnp
from jax import lax
from jax.experimental import pallas as pl
from jax.experimental.pallas import tpu as pltpu
from jax.sharding import Mesh
from jax.sharding import PartitionSpec as P

QUERY_HEADS = 128
KEY_VALUE_HEADS = 8
HEAD_SIZE = 128

WIDE = ("hi", "lo")
EVERY = ("hi", "lo", "narrow")


def apply_rotation(values, token_position):
    half = values.shape[-1] // 2
    freq = jnp.exp(jnp.arange(half, dtype=jnp.float32) * (-2.0 * math.log(500000.0) / HEAD_SIZE))
    angle = token_position * freq
    cosine = jnp.cos(angle)
    sine = jnp.sin(angle)
    first = values[..., :half]
    second = values[..., half:]
    return jnp.concatenate(
        [first * cosine - second * sine, second * cosine + first * sine], axis=-1
    )


def attend(query_vector, current_token, stored_keys, stored_values, channel_key_scale, lengths):
    owning_devices = query_vector.shape[0]
    slot_indices = stored_keys.shape[1]
    group_index = QUERY_HEADS // KEY_VALUE_HEADS
    inverse_scale = HEAD_SIZE ** (-0.5)
    token_position = lengths.astype(jnp.float32)
    rotated_query = apply_rotation(
        query_vector.astype(jnp.float32).reshape(
            owning_devices, KEY_VALUE_HEADS, group_index, HEAD_SIZE
        ),
        token_position[:, None, None, None],
    )
    rotated_key = apply_rotation(
        current_token[:, : KEY_VALUE_HEADS * HEAD_SIZE]
        .astype(jnp.float32)
        .reshape(owning_devices, KEY_VALUE_HEADS, HEAD_SIZE),
        token_position[:, None, None],
    )
    current_value = current_token[:, KEY_VALUE_HEADS * HEAD_SIZE :].reshape(
        owning_devices, KEY_VALUE_HEADS, HEAD_SIZE
    )
    stored_query = (
        rotated_query
        * channel_key_scale.reshape(owning_devices, KEY_VALUE_HEADS, 1, HEAD_SIZE)
        * inverse_scale
    ).astype(jnp.bfloat16)
    fresh_query = (rotated_query * inverse_scale).astype(jnp.bfloat16)
    fresh_key = rotated_key.astype(jnp.bfloat16)
    keys_divided = stored_keys.reshape(owning_devices, slot_indices, KEY_VALUE_HEADS, HEAD_SIZE)
    values_divided = stored_values.reshape(owning_devices, slot_indices, KEY_VALUE_HEADS, HEAD_SIZE)
    scores = jnp.einsum(
        "rgic,rpgc->rgip", stored_query, keys_divided, preferred_element_type=jnp.float32
    )
    fresh_score = jnp.sum(
        fresh_query.astype(jnp.float32) * fresh_key.astype(jnp.float32)[:, :, None, :], axis=-1
    )
    valid = (
        jnp.arange(slot_indices, dtype=jnp.int32)[None, None, None, :]
        < lengths[:, None, None, None]
    )
    masked = jnp.where(valid, scores, jnp.float32(-1e30))
    top = jnp.maximum(jnp.max(masked, axis=-1), fresh_score)
    exps = jnp.where(valid, jnp.exp(masked - top[..., None]), jnp.float32(0.0))
    fresh_exp = jnp.exp(fresh_score - top)
    total = jnp.sum(exps, axis=-1) + fresh_exp
    weights = exps.astype(jnp.bfloat16)
    fresh_weight = fresh_exp.astype(jnp.bfloat16)
    summed = jnp.einsum(
        "rgip,rpgc->rgic", weights, values_divided, preferred_element_type=jnp.float32
    )
    summed = (
        summed
        + fresh_weight.astype(jnp.float32)[..., None]
        * current_value.astype(jnp.float32)[:, :, None, :]
    )
    return (
        (summed / total[..., None])
        .astype(jnp.bfloat16)
        .reshape(owning_devices, QUERY_HEADS * HEAD_SIZE)
    )


def gather_wide(block):
    count = lax.axis_size(WIDE)
    me = lax.axis_index(WIDE)
    held = block
    depth = 0
    step = count // 2
    while step:
        other = lax.ppermute(held, WIDE, [(i, i ^ step) for i in range(count)])
        upper = (me & step) != 0
        held = jnp.stack(
            [jnp.where(upper, other, held), jnp.where(upper, held, other)], axis=depth
        )
        depth += 1
        step //= 2
    return held.reshape((count * block.shape[0],) + block.shape[1:])


def general_body(
    tokens,
    q_weight,
    key_value_weight,
    out_weight,
    stored_keys,
    stored_values,
    channel_key_scale,
    lengths,
):
    high = lax.axis_size("hi")
    low = lax.axis_size("lo")
    wide_count = high * low
    narrow = lax.axis_size("narrow")
    query_cols = q_weight.shape[1]
    row_width = query_cols + key_value_weight.shape[1]
    per_owner = stored_keys.shape[0]
    piece = gather_wide(tokens)
    partial_terms = jnp.concatenate(
        [
            jnp.dot(piece, q_weight, preferred_element_type=jnp.float32),
            jnp.dot(piece, key_value_weight, preferred_element_type=jnp.float32),
        ],
        axis=1,
    )
    received = lax.all_to_all(partial_terms, EVERY, split_axis=0, concat_axis=0, tiled=True)
    received = received.reshape(wide_count, narrow, per_owner, row_width)
    owned = jnp.sum(received, axis=1).astype(jnp.bfloat16).transpose(1, 0, 2)
    query_vector = owned[:, :, :query_cols].reshape(per_owner, wide_count * query_cols)
    current_token = owned[:, :, query_cols:].reshape(
        per_owner, wide_count * (row_width - query_cols)
    )
    attended = attend(
        query_vector, current_token, stored_keys, stored_values, channel_key_scale, lengths
    )
    depth = out_weight.shape[0]
    parts = attended.reshape(per_owner, narrow, depth).transpose(1, 0, 2)
    parts = jnp.broadcast_to(parts[None], (high, narrow, per_owner, depth))
    mine = lax.all_to_all(
        parts.reshape(high * narrow * per_owner, depth),
        ("hi", "narrow"),
        split_axis=0,
        concat_axis=0,
        tiled=True,
    ).reshape(high, 1, narrow * per_owner, depth)
    ordered = lax.all_gather(mine, "lo", axis=1, tiled=True)
    ordered = ordered.reshape(wide_count * narrow * per_owner, depth)
    terms = jnp.dot(ordered, out_weight, preferred_element_type=jnp.float32)
    return sum_narrow(terms).astype(jnp.bfloat16)


def sum_narrow(terms):
    narrow = lax.axis_size("narrow")
    me = lax.axis_index("narrow")
    rows = terms.shape[0] // narrow
    grouped = terms.reshape(narrow, rows, terms.shape[1])
    total = lax.dynamic_index_in_dim(grouped, me, 0, keepdims=False)
    for step in range(1, narrow):
        target = lax.rem(me + step, narrow)
        leaving = lax.dynamic_index_in_dim(grouped, target, 0, keepdims=False)
        total = total + lax.ppermute(
            leaving, "narrow", [(i, (i + step) % narrow) for i in range(narrow)]
        )
    return total


WHOLE = pl.BlockSpec(memory_space=pltpu.VMEM)
LANES = 128


def params(mebibytes):
    return pltpu.CompilerParams(vmem_limit_bytes=mebibytes << 20)


def join_kernel(a_ref, b_ref, _, o_ref):
    rows = a_ref.shape[0]
    o_ref[:rows] = a_ref[...]
    o_ref[rows:] = b_ref[...]


def join(a, b, ready):
    ready = pltpu.with_memory_space_constraint(ready, pltpu.VMEM)
    return pl.pallas_call(
        join_kernel,
        out_shape=jax.ShapeDtypeStruct((2 * a.shape[0],) + a.shape[1:], a.dtype),
        in_specs=[WHOLE] * 3,
        out_specs=WHOLE,
        compiler_params=params(2),
        cost_estimate=pl.CostEstimate(flops=0, bytes_accessed=8 * a.size, transcendentals=0),
        name="join_rows",
    )(a, b, ready)


def place_rows(piece_ref, turned, block, first, blocks):
    tiles = piece_ref.shape[1]
    for j in range(piece_ref.shape[0] // block):
        at = pl.multiple_of(blocks(j) * (block * tiles), block * tiles)
        turned[pl.ds(at, block * tiles), :] = (
            piece_ref[j * block : (j + 1) * block].reshape(block * tiles, LANES).astype(jnp.float32)
        )


def turned_rows(turned, rows, tiles, first, count):
    return jnp.concatenate(
        [turned[pl.ds(first + t, rows, stride=tiles), :] for t in range(count)], axis=1
    ).astype(jnp.bfloat16)


def opening_kernel(tokens_ref, length_ref, rows_ref, turn_ref, length_row_ref):
    rows, tiles, _ = rows_ref.shape
    values = tokens_ref[...].astype(jnp.float32)
    for r in range(rows):
        rows_ref[r] = jnp.concatenate(
            [values[r : r + 1, t * LANES : (t + 1) * LANES] for t in range(tiles)], axis=0
        ).astype(jnp.bfloat16)
    half = HEAD_SIZE // 2
    lane = lax.broadcasted_iota(jnp.int32, (1, HEAD_SIZE), 1)
    index = jnp.where(lane < half, lane, lane - half).astype(jnp.float32)
    freq = jnp.exp(index * (-2.0 * math.log(500000.0) / HEAD_SIZE))
    length = jnp.broadcast_to(length_ref[...], (1, HEAD_SIZE))
    angle = length.astype(jnp.float32) * freq
    sine = jnp.sin(angle)
    turn_ref[0:1] = jnp.cos(angle)
    turn_ref[1:2] = jnp.where(lane < half, -sine, sine)
    length_row_ref[...] = length


def opening(tokens, lengths):
    rows, width = tokens.shape
    return pl.pallas_call(
        opening_kernel,
        out_shape=(
            jax.ShapeDtypeStruct((rows, width // LANES, LANES), tokens.dtype),
            jax.ShapeDtypeStruct((2, HEAD_SIZE), jnp.float32),
            jax.ShapeDtypeStruct((1, HEAD_SIZE), jnp.int32),
        ),
        in_specs=[WHOLE] * 2,
        out_specs=(WHOLE,) * 3,
        compiler_params=params(2),
        cost_estimate=pl.CostEstimate(flops=0, bytes_accessed=4 * tokens.size, transcendentals=0),
        name="opening",
    )(tokens, lengths)


def load_kernel(first, weight_ref, after_ref, o_ref, sem):
    rows = o_ref.shape[0]
    copy = pltpu.make_async_copy(weight_ref.at[pl.ds(first, rows)], o_ref, sem)
    copy.start()
    copy.wait()


def load(weight, first, rows, after):
    weight = pltpu.with_memory_space_constraint(weight, pltpu.HBM)
    return pl.pallas_call(
        functools.partial(load_kernel, first),
        out_shape=pltpu.VMEM((rows, weight.shape[1]), weight.dtype),
        in_specs=[pl.BlockSpec(memory_space=pltpu.HBM), pl.BlockSpec(memory_space=pl.ANY)],
        out_specs=WHOLE,
        scratch_shapes=[pltpu.SemaphoreType.DMA],
        compiler_params=params(1),
        cost_estimate=pl.CostEstimate(
            flops=0, bytes_accessed=2 * rows * weight.shape[1], transcendentals=0
        ),
        name="load",
    )(weight, after)


def first_product_kernel(own_ref, other_ref, *refs):
    *q_refs, kv_ref, o_ref, turned = refs
    me = lax.axis_index(WIDE)
    pair = 2
    rows = 2 * own_ref.shape[0]
    tiles = own_ref.shape[1]
    count = rows // pair
    bits = count.bit_length() - 1

    def source(j, last):
        mask = last
        for bit in range(bits - 1):
            if j >> bit & 1:
                mask |= count >> (bit + 1)
        return me ^ mask

    place_rows(own_ref, turned, pair, 0, lambda j: source(j, 0))
    place_rows(other_ref, turned, pair, 0, lambda j: source(j, 1))
    group = 8
    deep = group * LANES
    q_cols, kv_cols = q_refs[0].shape[1], kv_ref.shape[1]
    totals = jnp.zeros((rows, q_cols), jnp.float32), jnp.zeros((rows, kv_cols), jnp.float32)
    base = 0
    for q_ref in q_refs:

        def step(k, carry):
            q_total, kv_total = carry
            x = turned_rows(turned, rows, tiles, (base // LANES) + k * group, group)
            at = pl.multiple_of(k * deep, deep)
            q_total = q_total + jnp.dot(
                x, q_ref[pl.ds(at, deep), :], preferred_element_type=jnp.float32
            )
            kv_total = kv_total + jnp.dot(
                x, kv_ref[pl.ds(base + at, deep), :], preferred_element_type=jnp.float32
            )
            return q_total, kv_total

        totals = lax.fori_loop(0, q_ref.shape[0] // deep, step, totals)
        base += q_ref.shape[0]
    q_total, kv_total = totals
    for r in range(rows):
        o_ref[r, :, :q_cols] = q_total[r : r + 1]
        o_ref[r, :, q_cols:] = kv_total[r : r + 1]


def first_product(own, other, q_parts, kv_weight):
    rows = 2 * own.shape[0]
    depth = kv_weight.shape[0]
    width = q_parts[0].shape[1] + kv_weight.shape[1]
    weights = [pltpu.with_memory_space_constraint(w, pltpu.VMEM) for w in (*q_parts, kv_weight)]
    return pl.pallas_call(
        first_product_kernel,
        out_shape=jax.ShapeDtypeStruct((rows, 1, width), jnp.float32),
        in_specs=[WHOLE] * (2 + len(weights)),
        out_specs=WHOLE,
        scratch_shapes=[pltpu.VMEM((rows * own.shape[1], LANES), jnp.float32)],
        compiler_params=params(6),
        cost_estimate=pl.CostEstimate(
            flops=2 * rows * depth * width,
            bytes_accessed=4 * own.size + 2 * depth * width,
            transcendentals=0,
        ),
        name="first_product",
    )(own, other, *weights)


def second_product_kernel(own_ref, other_ref, w_ref, keep_ref, send_ref, turned, w_buf, sems):
    low = lax.axis_index("lo")
    mine = lax.axis_index("narrow")
    chunks = w_buf.shape[0]
    deep = w_buf.shape[1]
    copies = [
        pltpu.make_async_copy(w_ref.at[pl.ds(c * deep, deep)], w_buf.at[c], sems.at[c])
        for c in range(chunks)
    ]
    for copy in copies:
        copy.start()
    pair = 2
    rows = 2 * own_ref.shape[0]
    tiles = own_ref.shape[1]
    place_rows(own_ref, turned, pair, 0, lambda j: 2 * j + low)
    place_rows(other_ref, turned, pair, 0, lambda j: 2 * j + (1 - low))
    group = deep // LANES
    total = jnp.zeros((rows, w_ref.shape[1]), jnp.float32)
    for c in range(chunks):
        x = turned_rows(turned, rows, tiles, c * group, group)
        copies[c].wait()
        total = total + jnp.dot(x, w_buf[c], preferred_element_type=jnp.float32)
    half = rows // 2
    lower = mine == 0
    keep_ref[...] = jnp.where(lower, total[:half], total[half:])
    send_ref[...] = jnp.where(lower, total[half:], total[:half])


def second_product(own, other, weight):
    rows = 2 * own.shape[0]
    cols = weight.shape[1]
    chunks = 8
    weight = pltpu.with_memory_space_constraint(weight, pltpu.HBM)
    half = jax.ShapeDtypeStruct((rows // 2, cols), jnp.float32)
    return pl.pallas_call(
        second_product_kernel,
        out_shape=(half, half),
        in_specs=[WHOLE, WHOLE, pl.BlockSpec(memory_space=pltpu.HBM)],
        out_specs=(WHOLE, WHOLE),
        scratch_shapes=[
            pltpu.VMEM((rows * own.shape[1], LANES), jnp.float32),
            pltpu.VMEM((chunks, weight.shape[0] // chunks, cols), weight.dtype),
            pltpu.SemaphoreType.DMA((chunks,)),
        ],
        compiler_params=params(24),
        cost_estimate=pl.CostEstimate(
            flops=2 * rows * weight.size, bytes_accessed=4 * own.size + 2 * weight.size, transcendentals=0
        ),
        name="second_product",
    )(own, other, weight)


def attention_kernel(length_ref, got_ref, keys_ref, values_ref, scale_ref, turn_ref, o_ref):
    copies, parts, per_part, _ = o_ref.shape
    heads_of = (got_ref.shape[2] - LANES) // LANES
    group = QUERY_HEADS // KEY_VALUE_HEADS
    sources = group // heads_of
    q_cols = heads_of * LANES
    slots = keys_ref.shape[1]
    inverse_scale = HEAD_SIZE ** (-0.5)
    cosine, sine = turn_ref[0:1], turn_ref[1:2]

    def rounded(w, at, size):
        total = got_ref[2 * w, :, at : at + size] + got_ref[2 * w + 1, :, at : at + size]
        return total.astype(jnp.bfloat16).astype(jnp.float32)

    def rotate(x):
        return x * cosine + pltpu.roll(x, HEAD_SIZE // 2, 1) * sine

    live = lax.broadcasted_iota(jnp.int32, (group, slots), 1) < jnp.concatenate(
        [length_ref[...]] * (slots // LANES), axis=1
    )
    for g in range(KEY_VALUE_HEADS):
        span = slice(g * HEAD_SIZE, (g + 1) * HEAD_SIZE)
        rows = []
        for w in range(g * sources, (g + 1) * sources):
            row = rounded(w, 0, q_cols)
            rows += [row[:, i * LANES : (i + 1) * LANES] for i in range(heads_of)]
        rotated = rotate(jnp.concatenate(rows, axis=0))
        fresh_key = rotate(rounded(g, q_cols, LANES)).astype(jnp.bfloat16).astype(jnp.float32)
        fresh_value = rounded(KEY_VALUE_HEADS + g, q_cols, LANES)
        cache_query = (rotated * scale_ref[:, span] * inverse_scale).astype(jnp.bfloat16)
        fresh_query = (rotated * inverse_scale).astype(jnp.bfloat16).astype(jnp.float32)
        scores = lax.dot_general(
            cache_query,
            keys_ref[0, :, span],
            (((1,), (1,)), ((), ())),
            preferred_element_type=jnp.float32,
        )
        fresh_score = jnp.sum(fresh_query * fresh_key, axis=-1, keepdims=True)
        masked = jnp.where(live, scores, jnp.float32(-1e30))
        top = jnp.maximum(jnp.max(masked, axis=-1, keepdims=True), fresh_score)
        exps = jnp.where(live, jnp.exp(masked - top), jnp.float32(0.0))
        fresh_exp = jnp.exp(fresh_score - top)
        total = jnp.sum(exps, axis=-1, keepdims=True) + fresh_exp
        summed = jnp.dot(
            exps.astype(jnp.bfloat16), values_ref[0, :, span], preferred_element_type=jnp.float32
        )
        summed = summed + fresh_exp.astype(jnp.bfloat16).astype(jnp.float32) * fresh_value
        attended = (summed / total).astype(jnp.bfloat16)
        part, at = divmod(g * group, per_part)
        for copy in range(copies):
            o_ref[copy, part, at : at + group, :] = attended


def attention(got, keys, values, scale, lengths, turn, copies, parts):
    keys = pltpu.with_memory_space_constraint(keys, pltpu.VMEM)
    values = pltpu.with_memory_space_constraint(values, pltpu.VMEM)
    return pl.pallas_call(
        attention_kernel,
        out_shape=jax.ShapeDtypeStruct((copies, parts, QUERY_HEADS // parts, HEAD_SIZE), jnp.bfloat16),
        in_specs=[WHOLE] * 6,
        out_specs=WHOLE,
        compiler_params=params(8),
        cost_estimate=pl.CostEstimate(
            flops=4 * QUERY_HEADS * keys.shape[1] * HEAD_SIZE,
            bytes_accessed=4 * keys.size,
            transcendentals=QUERY_HEADS * keys.shape[1],
        ),
        name="attention",
    )(lengths, got, keys, values, scale, turn)


def fits(tokens, q_weight, key_value_weight, stored_keys):
    return (
        lax.axis_size(WIDE) == 16
        and lax.axis_size("narrow") == 2
        and tokens.shape[0] == 2
        and stored_keys.shape[0] == 1
        and q_weight.shape[1] % 1024 == 0
        and key_value_weight.shape[1] == LANES
        and q_weight.shape[0] % 8192 == 0
    )


def tiled_body(
    tokens,
    q_weight,
    key_value_weight,
    out_weight,
    stored_keys,
    stored_values,
    channel_key_scale,
    lengths,
):
    count = lax.axis_size(WIDE)
    narrow = lax.axis_size("narrow")
    held, turn, lengths = opening(tokens, lengths.reshape(1, 1))
    eighth = q_weight.shape[0] // 8
    q_parts = []
    for step, first, last in ((8, 0, 2), (4, 2, 5), (2, 5, 8)):
        other = lax.ppermute(held, WIDE, [(i, i ^ step) for i in range(count)])
        part = load(q_weight, first * eighth, (last - first) * eighth, held)
        held = join(held, other, part)
        q_parts.append(part)
    other = lax.ppermute(held, WIDE, [(i, i ^ 1) for i in range(count)])
    kv_part = load(key_value_weight, 0, key_value_weight.shape[0], held)
    partial_terms = first_product(held, other, q_parts, kv_part)
    got = lax.all_to_all(partial_terms, EVERY, split_axis=0, concat_axis=0, tiled=True)
    attended = attention(
        got,
        stored_keys,
        stored_values,
        channel_key_scale,
        lengths,
        turn,
        lax.axis_size("hi"),
        narrow,
    )
    mine = lax.all_to_all(
        attended.reshape((-1,) + attended.shape[2:]),
        ("hi", "narrow"),
        split_axis=0,
        concat_axis=0,
        tiled=True,
    )
    other = lax.ppermute(mine, "lo", [(0, 1), (1, 0)])
    keep, send = second_product(mine, other, out_weight)
    return (keep + lax.ppermute(send, "narrow", [(0, 1), (1, 0)])).astype(jnp.bfloat16)


def body(*arguments):
    tokens, q_weight, key_value_weight, _, stored_keys = arguments[:5]
    if fits(tokens, q_weight, key_value_weight, stored_keys):
        return tiled_body(*arguments)
    return general_body(*arguments)


def solution(mesh):
    high, low, narrow = mesh.shape["wide"] // 2, 2, mesh.shape["narrow"]
    fine = Mesh(mesh.devices.reshape(high, low, narrow), EVERY)
    placed = (
        P(WIDE, "narrow"),
        P("narrow", WIDE),
        P("narrow", WIDE),
        P("narrow", WIDE),
        P(EVERY, None, None),
        P(EVERY, None, None),
        P(EVERY, None),
        P(EVERY),
    )
    return jax.shard_map(
        body, mesh=fine, in_specs=placed, out_specs=P("narrow", WIDE), check_vma=False
    )
```

```python
import functools
import math

import jax
import jax.numpy as jnp
from jax import lax
from jax.experimental import pallas as pl
from jax.experimental.pallas import tpu as pltpu
from jax.sharding import Mesh
from jax.sharding import PartitionSpec as P

QUERY_HEADS = 128
KEY_VALUE_HEADS = 8
HEAD_SIZE = 128

WIDE = ("hi", "lo")
EVERY = ("hi", "lo", "narrow")


def apply_rotation(values, token_position):
    half = values.shape[-1] // 2
    freq = jnp.exp(jnp.arange(half, dtype=jnp.float32) * (-2.0 * math.log(500000.0) / HEAD_SIZE))
    angle = token_position * freq
    cosine = jnp.cos(angle)
    sine = jnp.sin(angle)
    first = values[..., :half]
    second = values[..., half:]
    return jnp.concatenate(
        [first * cosine - second * sine, second * cosine + first * sine], axis=-1
    )


def attend(query_vector, current_token, stored_keys, stored_values, channel_key_scale, lengths):
    owning_devices = query_vector.shape[0]
    slot_indices = stored_keys.shape[1]
    group_index = QUERY_HEADS // KEY_VALUE_HEADS
    inverse_scale = HEAD_SIZE ** (-0.5)
    token_position = lengths.astype(jnp.float32)
    rotated_query = apply_rotation(
        query_vector.astype(jnp.float32).reshape(
            owning_devices, KEY_VALUE_HEADS, group_index, HEAD_SIZE
        ),
        token_position[:, None, None, None],
    )
    rotated_key = apply_rotation(
        current_token[:, : KEY_VALUE_HEADS * HEAD_SIZE]
        .astype(jnp.float32)
        .reshape(owning_devices, KEY_VALUE_HEADS, HEAD_SIZE),
        token_position[:, None, None],
    )
    current_value = current_token[:, KEY_VALUE_HEADS * HEAD_SIZE :].reshape(
        owning_devices, KEY_VALUE_HEADS, HEAD_SIZE
    )
    stored_query = (
        rotated_query
        * channel_key_scale.reshape(owning_devices, KEY_VALUE_HEADS, 1, HEAD_SIZE)
        * inverse_scale
    ).astype(jnp.bfloat16)
    fresh_query = (rotated_query * inverse_scale).astype(jnp.bfloat16)
    fresh_key = rotated_key.astype(jnp.bfloat16)
    keys_divided = stored_keys.reshape(owning_devices, slot_indices, KEY_VALUE_HEADS, HEAD_SIZE)
    values_divided = stored_values.reshape(owning_devices, slot_indices, KEY_VALUE_HEADS, HEAD_SIZE)
    scores = jnp.einsum(
        "rgic,rpgc->rgip", stored_query, keys_divided, preferred_element_type=jnp.float32
    )
    fresh_score = jnp.sum(
        fresh_query.astype(jnp.float32) * fresh_key.astype(jnp.float32)[:, :, None, :], axis=-1
    )
    valid = (
        jnp.arange(slot_indices, dtype=jnp.int32)[None, None, None, :]
        < lengths[:, None, None, None]
    )
    masked = jnp.where(valid, scores, jnp.float32(-1e30))
    top = jnp.maximum(jnp.max(masked, axis=-1), fresh_score)
    exps = jnp.where(valid, jnp.exp(masked - top[..., None]), jnp.float32(0.0))
    fresh_exp = jnp.exp(fresh_score - top)
    total = jnp.sum(exps, axis=-1) + fresh_exp
    weights = exps.astype(jnp.bfloat16)
    fresh_weight = fresh_exp.astype(jnp.bfloat16)
    summed = jnp.einsum(
        "rgip,rpgc->rgic", weights, values_divided, preferred_element_type=jnp.float32
    )
    summed = (
        summed
        + fresh_weight.astype(jnp.float32)[..., None]
        * current_value.astype(jnp.float32)[:, :, None, :]
    )
    return (
        (summed / total[..., None])
        .astype(jnp.bfloat16)
        .reshape(owning_devices, QUERY_HEADS * HEAD_SIZE)
    )


def gather_wide(block):
    count = lax.axis_size(WIDE)
    me = lax.axis_index(WIDE)
    held = block
    depth = 0
    step = count // 2
    while step:
        other = lax.ppermute(held, WIDE, [(i, i ^ step) for i in range(count)])
        upper = (me & step) != 0
        held = jnp.stack(
            [jnp.where(upper, other, held), jnp.where(upper, held, other)], axis=depth
        )
        depth += 1
        step //= 2
    return held.reshape((count * block.shape[0],) + block.shape[1:])


def general_body(
    tokens,
    q_weight,
    key_value_weight,
    out_weight,
    stored_keys,
    stored_values,
    channel_key_scale,
    lengths,
):
    high = lax.axis_size("hi")
    low = lax.axis_size("lo")
    wide_count = high * low
    narrow = lax.axis_size("narrow")
    query_cols = q_weight.shape[1]
    row_width = query_cols + key_value_weight.shape[1]
    per_owner = stored_keys.shape[0]
    piece = gather_wide(tokens)
    partial_terms = jnp.concatenate(
        [
            jnp.dot(piece, q_weight, preferred_element_type=jnp.float32),
            jnp.dot(piece, key_value_weight, preferred_element_type=jnp.float32),
        ],
        axis=1,
    )
    received = lax.all_to_all(partial_terms, EVERY, split_axis=0, concat_axis=0, tiled=True)
    received = received.reshape(wide_count, narrow, per_owner, row_width)
    owned = jnp.sum(received, axis=1).astype(jnp.bfloat16).transpose(1, 0, 2)
    query_vector = owned[:, :, :query_cols].reshape(per_owner, wide_count * query_cols)
    current_token = owned[:, :, query_cols:].reshape(
        per_owner, wide_count * (row_width - query_cols)
    )
    attended = attend(
        query_vector, current_token, stored_keys, stored_values, channel_key_scale, lengths
    )
    depth = out_weight.shape[0]
    parts = attended.reshape(per_owner, narrow, depth).transpose(1, 0, 2)
    parts = jnp.broadcast_to(parts[None], (high, narrow, per_owner, depth))
    mine = lax.all_to_all(
        parts.reshape(high * narrow * per_owner, depth),
        ("hi", "narrow"),
        split_axis=0,
        concat_axis=0,
        tiled=True,
    ).reshape(high, 1, narrow * per_owner, depth)
    ordered = lax.all_gather(mine, "lo", axis=1, tiled=True)
    ordered = ordered.reshape(wide_count * narrow * per_owner, depth)
    terms = jnp.dot(ordered, out_weight, preferred_element_type=jnp.float32)
    return sum_narrow(terms).astype(jnp.bfloat16)


def sum_narrow(terms):
    narrow = lax.axis_size("narrow")
    me = lax.axis_index("narrow")
    rows = terms.shape[0] // narrow
    grouped = terms.reshape(narrow, rows, terms.shape[1])
    total = lax.dynamic_index_in_dim(grouped, me, 0, keepdims=False)
    for step in range(1, narrow):
        target = lax.rem(me + step, narrow)
        leaving = lax.dynamic_index_in_dim(grouped, target, 0, keepdims=False)
        total = total + lax.ppermute(
            leaving, "narrow", [(i, (i + step) % narrow) for i in range(narrow)]
        )
    return total


WHOLE = pl.BlockSpec(memory_space=pltpu.VMEM)
LANES = 128


def params(mebibytes):
    return pltpu.CompilerParams(vmem_limit_bytes=mebibytes << 20)


def join_kernel(a_ref, b_ref, _, o_ref):
    rows = a_ref.shape[0]
    o_ref[:rows] = a_ref[...]
    o_ref[rows:] = b_ref[...]


def join(a, b, ready):
    ready = pltpu.with_memory_space_constraint(ready, pltpu.VMEM)
    return pl.pallas_call(
        join_kernel,
        out_shape=jax.ShapeDtypeStruct((2 * a.shape[0],) + a.shape[1:], a.dtype),
        in_specs=[WHOLE] * 3,
        out_specs=WHOLE,
        compiler_params=params(2),
        cost_estimate=pl.CostEstimate(flops=0, bytes_accessed=8 * a.size, transcendentals=0),
        name="join_rows",
    )(a, b, ready)


def place_rows(piece_ref, turned, block, first, blocks):
    tiles = piece_ref.shape[1]
    for j in range(piece_ref.shape[0] // block):
        at = pl.multiple_of(blocks(j) * (block * tiles), block * tiles)
        turned[pl.ds(at, block * tiles), :] = (
            piece_ref[j * block : (j + 1) * block].reshape(block * tiles, LANES).astype(jnp.float32)
        )


def turned_rows(turned, rows, tiles, first, count):
    return jnp.concatenate(
        [turned[pl.ds(first + t, rows, stride=tiles), :] for t in range(count)], axis=1
    ).astype(jnp.bfloat16)


def as_tiles(row, tiles):
    return jnp.concatenate(
        [row[:, t * LANES : (t + 1) * LANES] for t in range(tiles)], axis=0
    ).astype(jnp.bfloat16)


def opening_kernel(own_ref, other_ref, length_ref, _, rows_ref, turn_ref, length_row_ref):
    _, tiles, _ = rows_ref.shape
    rows = own_ref.shape[0]
    for i, ref in enumerate((own_ref, other_ref)):
        values = ref[...].astype(jnp.float32)
        for r in range(rows):
            rows_ref[i * rows + r] = as_tiles(values[r : r + 1], tiles)
    half = HEAD_SIZE // 2
    lane = lax.broadcasted_iota(jnp.int32, (1, HEAD_SIZE), 1)
    index = jnp.where(lane < half, lane, lane - half).astype(jnp.float32)
    freq = jnp.exp(index * (-2.0 * math.log(500000.0) / HEAD_SIZE))
    length = jnp.full((1, HEAD_SIZE), length_ref[0], jnp.int32)
    angle = length.astype(jnp.float32) * freq
    sine = jnp.sin(angle)
    turn_ref[0:1] = jnp.cos(angle)
    turn_ref[1:2] = jnp.where(lane < half, -sine, sine)
    length_row_ref[...] = length


def opening(tokens, other, lengths, ready):
    rows, width = tokens.shape
    ready = pltpu.with_memory_space_constraint(ready, pltpu.VMEM)
    return pl.pallas_call(
        opening_kernel,
        out_shape=(
            jax.ShapeDtypeStruct((2 * rows, width // LANES, LANES), tokens.dtype),
            jax.ShapeDtypeStruct((2, HEAD_SIZE), jnp.float32),
            jax.ShapeDtypeStruct((1, HEAD_SIZE), jnp.int32),
        ),
        in_specs=[WHOLE, WHOLE, pl.BlockSpec(memory_space=pltpu.SMEM), WHOLE],
        out_specs=(WHOLE,) * 3,
        compiler_params=params(2),
        cost_estimate=pl.CostEstimate(flops=0, bytes_accessed=8 * tokens.size, transcendentals=0),
        name="opening",
    )(tokens, other, lengths, ready)


def load_kernel(first, weight_ref, *refs):
    *_, o_ref, sem = refs
    rows = o_ref.shape[0]
    copy = pltpu.make_async_copy(weight_ref.at[pl.ds(first, rows)], o_ref, sem)
    copy.start()
    copy.wait()


def load(weight, first, rows, *after):
    weight = pltpu.with_memory_space_constraint(weight, pltpu.HBM)
    return pl.pallas_call(
        functools.partial(load_kernel, first),
        out_shape=pltpu.VMEM((rows, weight.shape[1]), weight.dtype),
        in_specs=[pl.BlockSpec(memory_space=pltpu.HBM)]
        + [pl.BlockSpec(memory_space=pl.ANY)] * len(after),
        out_specs=WHOLE,
        scratch_shapes=[pltpu.SemaphoreType.DMA],
        compiler_params=params(1),
        cost_estimate=pl.CostEstimate(
            flops=0, bytes_accessed=2 * rows * weight.shape[1], transcendentals=0
        ),
        name="load",
    )(weight, *after)


def first_product_kernel(own_ref, other_ref, *refs):
    *q_refs, kv_ref, o_ref, turned = refs
    me = lax.axis_index(WIDE)
    pair = 2
    rows = 2 * own_ref.shape[0]
    tiles = own_ref.shape[1]
    count = rows // pair
    bits = count.bit_length() - 1

    def source(j, last):
        mask = last
        for bit in range(bits - 1):
            if j >> bit & 1:
                mask |= count >> (bit + 1)
        return me ^ mask

    place_rows(own_ref, turned, pair, 0, lambda j: source(j, 0))
    place_rows(other_ref, turned, pair, 0, lambda j: source(j, 1))
    group = 8
    deep = group * LANES
    q_cols, kv_cols = q_refs[0].shape[1], kv_ref.shape[1]
    totals = jnp.zeros((rows, q_cols), jnp.float32), jnp.zeros((rows, kv_cols), jnp.float32)
    base = 0
    for q_ref in q_refs:

        def step(k, carry):
            q_total, kv_total = carry
            x = turned_rows(turned, rows, tiles, (base // LANES) + k * group, group)
            at = pl.multiple_of(k * deep, deep)
            q_total = q_total + jnp.dot(
                x, q_ref[pl.ds(at, deep), :], preferred_element_type=jnp.float32
            )
            kv_total = kv_total + jnp.dot(
                x, kv_ref[pl.ds(base + at, deep), :], preferred_element_type=jnp.float32
            )
            return q_total, kv_total

        totals = lax.fori_loop(0, q_ref.shape[0] // deep, step, totals)
        base += q_ref.shape[0]
    q_total, kv_total = totals
    for r in range(rows):
        o_ref[r, :, :q_cols] = q_total[r : r + 1]
        o_ref[r, :, q_cols:] = kv_total[r : r + 1]


def first_product(own, other, q_parts, kv_weight):
    rows = 2 * own.shape[0]
    depth = kv_weight.shape[0]
    width = q_parts[0].shape[1] + kv_weight.shape[1]
    weights = [pltpu.with_memory_space_constraint(w, pltpu.VMEM) for w in (*q_parts, kv_weight)]
    return pl.pallas_call(
        first_product_kernel,
        out_shape=jax.ShapeDtypeStruct((rows, 1, width), jnp.float32),
        in_specs=[WHOLE] * (2 + len(weights)),
        out_specs=WHOLE,
        scratch_shapes=[pltpu.VMEM((rows * own.shape[1], LANES), jnp.float32)],
        compiler_params=params(6),
        cost_estimate=pl.CostEstimate(
            flops=2 * rows * depth * width,
            bytes_accessed=4 * own.size + 2 * depth * width,
            transcendentals=0,
        ),
        name="first_product",
    )(own, other, *weights)


def second_product_kernel(own_ref, other_ref, w_ref, keep_ref, send_ref, turned, w_buf, sems):
    low = lax.axis_index("lo")
    mine = lax.axis_index("narrow")
    chunks = w_buf.shape[0]
    deep = w_buf.shape[1]
    copies = [
        pltpu.make_async_copy(w_ref.at[pl.ds(c * deep, deep)], w_buf.at[c], sems.at[c])
        for c in range(chunks)
    ]
    for copy in copies:
        copy.start()
    pair = 2
    rows = 2 * own_ref.shape[0]
    tiles = own_ref.shape[1]
    place_rows(own_ref, turned, pair, 0, lambda j: 2 * j + low)
    place_rows(other_ref, turned, pair, 0, lambda j: 2 * j + (1 - low))
    group = deep // LANES
    total = jnp.zeros((rows, w_ref.shape[1]), jnp.float32)
    for c in range(chunks):
        x = turned_rows(turned, rows, tiles, c * group, group)
        copies[c].wait()
        total = total + jnp.dot(x, w_buf[c], preferred_element_type=jnp.float32)
    half = rows // 2
    lower = mine == 0
    keep_ref[...] = jnp.where(lower, total[:half], total[half:])
    send_ref[...] = jnp.where(lower, total[half:], total[:half])


def second_product(own, other, weight):
    rows = 2 * own.shape[0]
    cols = weight.shape[1]
    chunks = 8
    weight = pltpu.with_memory_space_constraint(weight, pltpu.HBM)
    half = jax.ShapeDtypeStruct((rows // 2, cols), jnp.float32)
    return pl.pallas_call(
        second_product_kernel,
        out_shape=(half, half),
        in_specs=[WHOLE, WHOLE, pl.BlockSpec(memory_space=pltpu.HBM)],
        out_specs=(WHOLE, WHOLE),
        scratch_shapes=[
            pltpu.VMEM((rows * own.shape[1], LANES), jnp.float32),
            pltpu.VMEM((chunks, weight.shape[0] // chunks, cols), weight.dtype),
            pltpu.SemaphoreType.DMA((chunks,)),
        ],
        compiler_params=params(24),
        cost_estimate=pl.CostEstimate(
            flops=2 * rows * weight.size, bytes_accessed=4 * own.size + 2 * weight.size, transcendentals=0
        ),
        name="second_product",
    )(own, other, weight)


def attention_kernel(length_ref, got_ref, keys_ref, values_ref, scale_ref, turn_ref, o_ref):
    copies, parts, per_part, _ = o_ref.shape
    heads_of = (got_ref.shape[2] - LANES) // LANES
    group = QUERY_HEADS // KEY_VALUE_HEADS
    sources = group // heads_of
    q_cols = heads_of * LANES
    slots = keys_ref.shape[1]
    inverse_scale = HEAD_SIZE ** (-0.5)
    cosine, sine = turn_ref[0:1], turn_ref[1:2]

    def rounded(w, at, size):
        total = got_ref[2 * w, :, at : at + size] + got_ref[2 * w + 1, :, at : at + size]
        return total.astype(jnp.bfloat16).astype(jnp.float32)

    def rotate(x):
        return x * cosine + pltpu.roll(x, HEAD_SIZE // 2, 1) * sine

    live = lax.broadcasted_iota(jnp.int32, (group, slots), 1) < jnp.concatenate(
        [length_ref[...]] * (slots // LANES), axis=1
    )
    for g in range(KEY_VALUE_HEADS):
        span = slice(g * HEAD_SIZE, (g + 1) * HEAD_SIZE)
        rows = []
        for w in range(g * sources, (g + 1) * sources):
            rows.append(rounded(w, 0, q_cols).reshape(heads_of, LANES))
        rotated = rotate(jnp.concatenate(rows, axis=0))
        fresh_key = rotate(rounded(g, q_cols, LANES)).astype(jnp.bfloat16).astype(jnp.float32)
        fresh_value = rounded(KEY_VALUE_HEADS + g, q_cols, LANES)
        cache_query = (rotated * scale_ref[:, span] * inverse_scale).astype(jnp.bfloat16)
        fresh_query = (rotated * inverse_scale).astype(jnp.bfloat16).astype(jnp.float32)
        scores = lax.dot_general(
            cache_query,
            keys_ref[0, :, span],
            (((1,), (1,)), ((), ())),
            preferred_element_type=jnp.float32,
        )
        fresh_score = jnp.sum(fresh_query * fresh_key, axis=-1, keepdims=True)
        masked = jnp.where(live, scores, jnp.float32(-1e30))
        top = jnp.maximum(jnp.max(masked, axis=-1, keepdims=True), fresh_score)
        exps = jnp.where(live, jnp.exp(masked - top), jnp.float32(0.0))
        fresh_exp = jnp.exp(fresh_score - top)
        total = jnp.sum(exps, axis=-1, keepdims=True) + fresh_exp
        summed = jnp.dot(
            exps.astype(jnp.bfloat16), values_ref[0, :, span], preferred_element_type=jnp.float32
        )
        summed = summed + fresh_exp.astype(jnp.bfloat16).astype(jnp.float32) * fresh_value
        attended = (summed / total).astype(jnp.bfloat16)
        part, at = divmod(g * group, per_part)
        for copy in range(copies):
            o_ref[copy, part, at : at + group, :] = attended


def attention(got, keys, values, scale, lengths, turn, copies, parts):
    keys = pltpu.with_memory_space_constraint(keys, pltpu.VMEM)
    values = pltpu.with_memory_space_constraint(values, pltpu.VMEM)
    return pl.pallas_call(
        attention_kernel,
        out_shape=jax.ShapeDtypeStruct((copies, parts, QUERY_HEADS // parts, HEAD_SIZE), jnp.bfloat16),
        in_specs=[WHOLE] * 6,
        out_specs=WHOLE,
        compiler_params=params(8),
        cost_estimate=pl.CostEstimate(
            flops=4 * QUERY_HEADS * keys.shape[1] * HEAD_SIZE,
            bytes_accessed=4 * keys.size,
            transcendentals=QUERY_HEADS * keys.shape[1],
        ),
        name="attention",
    )(lengths, got, keys, values, scale, turn)


def fits(tokens, q_weight, key_value_weight, stored_keys):
    return (
        lax.axis_size(WIDE) == 16
        and lax.axis_size("narrow") == 2
        and tokens.shape[0] == 2
        and stored_keys.shape[0] == 1
        and q_weight.shape[1] % 1024 == 0
        and key_value_weight.shape[1] == LANES
        and q_weight.shape[0] % 8192 == 0
    )


def tiled_body(
    tokens,
    q_weight,
    key_value_weight,
    out_weight,
    stored_keys,
    stored_values,
    channel_key_scale,
    lengths,
):
    count = lax.axis_size(WIDE)
    narrow = lax.axis_size("narrow")
    eighth = q_weight.shape[0] // 8
    q_parts = []
    held, held_rows = tokens, []
    for step, first, last in ((8, 0, 2), (4, 2, 5), (2, 5, 8)):
        other = lax.ppermute(held, WIDE, [(i, i ^ step) for i in range(count)])
        part = load(q_weight, first * eighth, (last - first) * eighth, *held_rows)
        if held_rows:
            held = join(held, other, part)
        else:
            held, turn, lengths = opening(tokens, other, lengths, part)
        q_parts.append(part)
        held_rows = [held]
    other = lax.ppermute(held, WIDE, [(i, i ^ 1) for i in range(count)])
    kv_part = load(key_value_weight, 0, key_value_weight.shape[0], held)
    partial_terms = first_product(held, other, q_parts, kv_part)
    got = lax.all_to_all(partial_terms, EVERY, split_axis=0, concat_axis=0, tiled=True)
    attended = attention(
        got,
        stored_keys,
        stored_values,
        channel_key_scale,
        lengths,
        turn,
        lax.axis_size("hi"),
        narrow,
    )
    mine = lax.all_to_all(
        attended.reshape((-1,) + attended.shape[2:]),
        ("hi", "narrow"),
        split_axis=0,
        concat_axis=0,
        tiled=True,
    )
    other = lax.ppermute(mine, "lo", [(0, 1), (1, 0)])
    keep, send = second_product(mine, other, out_weight)
    return (keep + lax.ppermute(send, "narrow", [(0, 1), (1, 0)])).astype(jnp.bfloat16)


def body(*arguments):
    tokens, q_weight, key_value_weight, _, stored_keys = arguments[:5]
    if fits(tokens, q_weight, key_value_weight, stored_keys):
        return tiled_body(*arguments)
    return general_body(*arguments)


def solution(mesh):
    high, low, narrow = mesh.shape["wide"] // 2, 2, mesh.shape["narrow"]
    fine = Mesh(mesh.devices.reshape(high, low, narrow), EVERY)
    placed = (
        P(WIDE, "narrow"),
        P("narrow", WIDE),
        P("narrow", WIDE),
        P("narrow", WIDE),
        P(EVERY, None, None),
        P(EVERY, None, None),
        P(EVERY, None),
        P(EVERY),
    )
    return jax.shard_map(
        body, mesh=fine, in_specs=placed, out_specs=P("narrow", WIDE), check_vma=False
    )
```

```python
import functools
import math

import jax
import jax.numpy as jnp
from jax import lax
from jax.experimental import pallas as pl
from jax.experimental.pallas import tpu as pltpu
from jax.sharding import Mesh
from jax.sharding import PartitionSpec as P

QUERY_HEADS = 128
KEY_VALUE_HEADS = 8
HEAD_SIZE = 128

WIDE = ("hi", "lo")
EVERY = ("hi", "lo", "narrow")


def apply_rotation(values, token_position):
    half = values.shape[-1] // 2
    freq = jnp.exp(jnp.arange(half, dtype=jnp.float32) * (-2.0 * math.log(500000.0) / HEAD_SIZE))
    angle = token_position * freq
    cosine = jnp.cos(angle)
    sine = jnp.sin(angle)
    first = values[..., :half]
    second = values[..., half:]
    return jnp.concatenate(
        [first * cosine - second * sine, second * cosine + first * sine], axis=-1
    )


def attend(query_vector, current_token, stored_keys, stored_values, channel_key_scale, lengths):
    owning_devices = query_vector.shape[0]
    slot_indices = stored_keys.shape[1]
    group_index = QUERY_HEADS // KEY_VALUE_HEADS
    inverse_scale = HEAD_SIZE ** (-0.5)
    token_position = lengths.astype(jnp.float32)
    rotated_query = apply_rotation(
        query_vector.astype(jnp.float32).reshape(
            owning_devices, KEY_VALUE_HEADS, group_index, HEAD_SIZE
        ),
        token_position[:, None, None, None],
    )
    rotated_key = apply_rotation(
        current_token[:, : KEY_VALUE_HEADS * HEAD_SIZE]
        .astype(jnp.float32)
        .reshape(owning_devices, KEY_VALUE_HEADS, HEAD_SIZE),
        token_position[:, None, None],
    )
    current_value = current_token[:, KEY_VALUE_HEADS * HEAD_SIZE :].reshape(
        owning_devices, KEY_VALUE_HEADS, HEAD_SIZE
    )
    stored_query = (
        rotated_query
        * channel_key_scale.reshape(owning_devices, KEY_VALUE_HEADS, 1, HEAD_SIZE)
        * inverse_scale
    ).astype(jnp.bfloat16)
    fresh_query = (rotated_query * inverse_scale).astype(jnp.bfloat16)
    fresh_key = rotated_key.astype(jnp.bfloat16)
    keys_divided = stored_keys.reshape(owning_devices, slot_indices, KEY_VALUE_HEADS, HEAD_SIZE)
    values_divided = stored_values.reshape(owning_devices, slot_indices, KEY_VALUE_HEADS, HEAD_SIZE)
    scores = jnp.einsum(
        "rgic,rpgc->rgip", stored_query, keys_divided, preferred_element_type=jnp.float32
    )
    fresh_score = jnp.sum(
        fresh_query.astype(jnp.float32) * fresh_key.astype(jnp.float32)[:, :, None, :], axis=-1
    )
    valid = (
        jnp.arange(slot_indices, dtype=jnp.int32)[None, None, None, :]
        < lengths[:, None, None, None]
    )
    masked = jnp.where(valid, scores, jnp.float32(-1e30))
    top = jnp.maximum(jnp.max(masked, axis=-1), fresh_score)
    exps = jnp.where(valid, jnp.exp(masked - top[..., None]), jnp.float32(0.0))
    fresh_exp = jnp.exp(fresh_score - top)
    total = jnp.sum(exps, axis=-1) + fresh_exp
    weights = exps.astype(jnp.bfloat16)
    fresh_weight = fresh_exp.astype(jnp.bfloat16)
    summed = jnp.einsum(
        "rgip,rpgc->rgic", weights, values_divided, preferred_element_type=jnp.float32
    )
    summed = (
        summed
        + fresh_weight.astype(jnp.float32)[..., None]
        * current_value.astype(jnp.float32)[:, :, None, :]
    )
    return (
        (summed / total[..., None])
        .astype(jnp.bfloat16)
        .reshape(owning_devices, QUERY_HEADS * HEAD_SIZE)
    )


def gather_wide(block):
    count = lax.axis_size(WIDE)
    me = lax.axis_index(WIDE)
    held = block
    depth = 0
    step = count // 2
    while step:
        other = lax.ppermute(held, WIDE, [(i, i ^ step) for i in range(count)])
        upper = (me & step) != 0
        held = jnp.stack(
            [jnp.where(upper, other, held), jnp.where(upper, held, other)], axis=depth
        )
        depth += 1
        step //= 2
    return held.reshape((count * block.shape[0],) + block.shape[1:])


def general_body(
    tokens,
    q_weight,
    key_value_weight,
    out_weight,
    stored_keys,
    stored_values,
    channel_key_scale,
    lengths,
):
    high = lax.axis_size("hi")
    low = lax.axis_size("lo")
    wide_count = high * low
    narrow = lax.axis_size("narrow")
    query_cols = q_weight.shape[1]
    row_width = query_cols + key_value_weight.shape[1]
    per_owner = stored_keys.shape[0]
    piece = gather_wide(tokens)
    partial_terms = jnp.concatenate(
        [
            jnp.dot(piece, q_weight, preferred_element_type=jnp.float32),
            jnp.dot(piece, key_value_weight, preferred_element_type=jnp.float32),
        ],
        axis=1,
    )
    received = lax.all_to_all(partial_terms, EVERY, split_axis=0, concat_axis=0, tiled=True)
    received = received.reshape(wide_count, narrow, per_owner, row_width)
    owned = jnp.sum(received, axis=1).astype(jnp.bfloat16).transpose(1, 0, 2)
    query_vector = owned[:, :, :query_cols].reshape(per_owner, wide_count * query_cols)
    current_token = owned[:, :, query_cols:].reshape(
        per_owner, wide_count * (row_width - query_cols)
    )
    attended = attend(
        query_vector, current_token, stored_keys, stored_values, channel_key_scale, lengths
    )
    depth = out_weight.shape[0]
    parts = attended.reshape(per_owner, narrow, depth).transpose(1, 0, 2)
    parts = jnp.broadcast_to(parts[None], (high, narrow, per_owner, depth))
    mine = lax.all_to_all(
        parts.reshape(high * narrow * per_owner, depth),
        ("hi", "narrow"),
        split_axis=0,
        concat_axis=0,
        tiled=True,
    ).reshape(high, 1, narrow * per_owner, depth)
    ordered = lax.all_gather(mine, "lo", axis=1, tiled=True)
    ordered = ordered.reshape(wide_count * narrow * per_owner, depth)
    terms = jnp.dot(ordered, out_weight, preferred_element_type=jnp.float32)
    return sum_narrow(terms).astype(jnp.bfloat16)


def sum_narrow(terms):
    narrow = lax.axis_size("narrow")
    me = lax.axis_index("narrow")
    rows = terms.shape[0] // narrow
    grouped = terms.reshape(narrow, rows, terms.shape[1])
    total = lax.dynamic_index_in_dim(grouped, me, 0, keepdims=False)
    for step in range(1, narrow):
        target = lax.rem(me + step, narrow)
        leaving = lax.dynamic_index_in_dim(grouped, target, 0, keepdims=False)
        total = total + lax.ppermute(
            leaving, "narrow", [(i, (i + step) % narrow) for i in range(narrow)]
        )
    return total


WHOLE = pl.BlockSpec(memory_space=pltpu.VMEM)
LANES = 128


def params(mebibytes):
    return pltpu.CompilerParams(vmem_limit_bytes=mebibytes << 20)


def join_kernel(a_ref, b_ref, _, o_ref):
    rows = a_ref.shape[0]
    o_ref[:rows] = a_ref[...]
    o_ref[rows:] = b_ref[...]


def join(a, b, ready):
    ready = pltpu.with_memory_space_constraint(ready, pltpu.VMEM)
    return pl.pallas_call(
        join_kernel,
        out_shape=jax.ShapeDtypeStruct((2 * a.shape[0],) + a.shape[1:], a.dtype),
        in_specs=[WHOLE] * 3,
        out_specs=WHOLE,
        compiler_params=params(2),
        cost_estimate=pl.CostEstimate(flops=0, bytes_accessed=8 * a.size, transcendentals=0),
        name="join_rows",
    )(a, b, ready)


def place_rows(piece_ref, turned, block, first, blocks):
    tiles = piece_ref.shape[1]
    for j in range(piece_ref.shape[0] // block):
        at = pl.multiple_of(blocks(j) * (block * tiles), block * tiles)
        turned[pl.ds(at, block * tiles), :] = (
            piece_ref[j * block : (j + 1) * block].reshape(block * tiles, LANES).astype(jnp.float32)
        )


def turned_rows(turned, rows, tiles, first, count):
    return jnp.concatenate(
        [turned[pl.ds(first + t, rows, stride=tiles), :] for t in range(count)], axis=1
    ).astype(jnp.bfloat16)


def as_tiles(row, tiles):
    return jnp.concatenate(
        [row[:, t * LANES : (t + 1) * LANES] for t in range(tiles)], axis=0
    ).astype(jnp.bfloat16)


def opening_kernel(own_ref, other_ref, length_ref, _, rows_ref, turn_ref, length_row_ref):
    _, tiles, _ = rows_ref.shape
    rows = own_ref.shape[0]
    for i, ref in enumerate((own_ref, other_ref)):
        values = ref[...].astype(jnp.float32)
        for r in range(rows):
            rows_ref[i * rows + r] = as_tiles(values[r : r + 1], tiles)
    half = HEAD_SIZE // 2
    lane = lax.broadcasted_iota(jnp.int32, (1, HEAD_SIZE), 1)
    index = jnp.where(lane < half, lane, lane - half).astype(jnp.float32)
    freq = jnp.exp(index * (-2.0 * math.log(500000.0) / HEAD_SIZE))
    length = jnp.full((1, HEAD_SIZE), length_ref[0], jnp.int32)
    angle = length.astype(jnp.float32) * freq
    sine = jnp.sin(angle)
    turn_ref[0:1] = jnp.cos(angle)
    turn_ref[1:2] = jnp.where(lane < half, -sine, sine)
    length_row_ref[...] = length


def opening(tokens, other, lengths, ready):
    rows, width = tokens.shape
    ready = pltpu.with_memory_space_constraint(ready, pltpu.VMEM)
    return pl.pallas_call(
        opening_kernel,
        out_shape=(
            jax.ShapeDtypeStruct((2 * rows, width // LANES, LANES), tokens.dtype),
            jax.ShapeDtypeStruct((2, HEAD_SIZE), jnp.float32),
            jax.ShapeDtypeStruct((1, HEAD_SIZE), jnp.int32),
        ),
        in_specs=[WHOLE, WHOLE, pl.BlockSpec(memory_space=pltpu.SMEM), WHOLE],
        out_specs=(WHOLE,) * 3,
        compiler_params=params(2),
        cost_estimate=pl.CostEstimate(flops=0, bytes_accessed=8 * tokens.size, transcendentals=0),
        name="opening",
    )(tokens, other, lengths, ready)


def load_kernel(first, weight_ref, *refs):
    *_, o_ref, sem = refs
    rows = o_ref.shape[0]
    copy = pltpu.make_async_copy(weight_ref.at[pl.ds(first, rows)], o_ref, sem)
    copy.start()
    copy.wait()


def load(weight, first, rows, *after):
    weight = pltpu.with_memory_space_constraint(weight, pltpu.HBM)
    return pl.pallas_call(
        functools.partial(load_kernel, first),
        out_shape=pltpu.VMEM((rows, weight.shape[1]), weight.dtype),
        in_specs=[pl.BlockSpec(memory_space=pltpu.HBM)]
        + [pl.BlockSpec(memory_space=pl.ANY)] * len(after),
        out_specs=WHOLE,
        scratch_shapes=[pltpu.SemaphoreType.DMA],
        compiler_params=params(1),
        cost_estimate=pl.CostEstimate(
            flops=0, bytes_accessed=2 * rows * weight.shape[1], transcendentals=0
        ),
        name="load",
    )(weight, *after)


def first_product_kernel(own_ref, other_ref, *refs):
    *q_refs, kv_ref, o_ref, turned = refs
    me = lax.axis_index(WIDE)
    pair = 2
    rows = 2 * own_ref.shape[0]
    tiles = own_ref.shape[1]
    count = rows // pair
    bits = count.bit_length() - 1

    def source(j, last):
        mask = last
        for bit in range(bits - 1):
            if j >> bit & 1:
                mask |= count >> (bit + 1)
        return me ^ mask

    place_rows(own_ref, turned, pair, 0, lambda j: source(j, 0))
    place_rows(other_ref, turned, pair, 0, lambda j: source(j, 1))
    group = 8
    deep = group * LANES
    q_cols, kv_cols = q_refs[0].shape[1], kv_ref.shape[1]
    totals = jnp.zeros((rows, q_cols), jnp.float32), jnp.zeros((rows, kv_cols), jnp.float32)
    base = 0
    for q_ref in q_refs:

        def step(k, carry):
            q_total, kv_total = carry
            x = turned_rows(turned, rows, tiles, (base // LANES) + k * group, group)
            at = pl.multiple_of(k * deep, deep)
            q_total = q_total + jnp.dot(
                x, q_ref[pl.ds(at, deep), :], preferred_element_type=jnp.float32
            )
            kv_total = kv_total + jnp.dot(
                x, kv_ref[pl.ds(base + at, deep), :], preferred_element_type=jnp.float32
            )
            return q_total, kv_total

        totals = lax.fori_loop(0, q_ref.shape[0] // deep, step, totals)
        base += q_ref.shape[0]
    q_total, kv_total = totals
    for r in range(rows):
        o_ref[r, :, :q_cols] = q_total[r : r + 1]
        o_ref[r, :, q_cols:] = kv_total[r : r + 1]


def first_product(own, other, q_parts, kv_weight):
    rows = 2 * own.shape[0]
    depth = kv_weight.shape[0]
    width = q_parts[0].shape[1] + kv_weight.shape[1]
    weights = [pltpu.with_memory_space_constraint(w, pltpu.VMEM) for w in (*q_parts, kv_weight)]
    return pl.pallas_call(
        first_product_kernel,
        out_shape=jax.ShapeDtypeStruct((rows, 1, width), jnp.float32),
        in_specs=[WHOLE] * (2 + len(weights)),
        out_specs=WHOLE,
        scratch_shapes=[pltpu.VMEM((rows * own.shape[1], LANES), jnp.float32)],
        compiler_params=params(6),
        cost_estimate=pl.CostEstimate(
            flops=2 * rows * depth * width,
            bytes_accessed=4 * own.size + 2 * depth * width,
            transcendentals=0,
        ),
        name="first_product",
    )(own, other, *weights)


def second_product_kernel(own_ref, other_ref, w_ref, *refs):
    *parts, keep_ref, send_ref, turned, w_buf, sems = refs
    low = lax.axis_index("lo")
    mine = lax.axis_index("narrow")
    chunks = w_buf.shape[0]
    deep = w_buf.shape[1]
    base = sum(part.shape[0] for part in parts)
    copies = [
        pltpu.make_async_copy(w_ref.at[pl.ds(base + c * deep, deep)], w_buf.at[c], sems.at[c])
        for c in range(chunks)
    ]
    for copy in copies:
        copy.start()
    pair = 2
    rows = 2 * own_ref.shape[0]
    tiles = own_ref.shape[1]
    place_rows(own_ref, turned, pair, 0, lambda j: 2 * j + low)
    place_rows(other_ref, turned, pair, 0, lambda j: 2 * j + (1 - low))
    total = jnp.zeros((rows, w_ref.shape[1]), jnp.float32)
    at = 0
    for part in parts:
        x = turned_rows(turned, rows, tiles, at // LANES, part.shape[0] // LANES)
        total = total + jnp.dot(x, part[...], preferred_element_type=jnp.float32)
        at += part.shape[0]
    for c in range(chunks):
        x = turned_rows(turned, rows, tiles, (at + c * deep) // LANES, deep // LANES)
        copies[c].wait()
        total = total + jnp.dot(x, w_buf[c], preferred_element_type=jnp.float32)
    half = rows // 2
    lower = mine == 0
    keep_ref[...] = jnp.where(lower, total[:half], total[half:])
    send_ref[...] = jnp.where(lower, total[half:], total[:half])


def second_product(own, other, weight, parts):
    rows = 2 * own.shape[0]
    cols = weight.shape[1]
    deep = 512
    chunks = (weight.shape[0] - sum(part.shape[0] for part in parts)) // deep
    weight = pltpu.with_memory_space_constraint(weight, pltpu.HBM)
    parts = [pltpu.with_memory_space_constraint(part, pltpu.VMEM) for part in parts]
    half = jax.ShapeDtypeStruct((rows // 2, cols), jnp.float32)
    return pl.pallas_call(
        second_product_kernel,
        out_shape=(half, half),
        in_specs=[WHOLE, WHOLE, pl.BlockSpec(memory_space=pltpu.HBM)] + [WHOLE] * len(parts),
        out_specs=(WHOLE, WHOLE),
        scratch_shapes=[
            pltpu.VMEM((rows * own.shape[1], LANES), jnp.float32),
            pltpu.VMEM((chunks, deep, cols), weight.dtype),
            pltpu.SemaphoreType.DMA((chunks,)),
        ],
        compiler_params=params(24),
        cost_estimate=pl.CostEstimate(
            flops=2 * rows * weight.size, bytes_accessed=4 * own.size + 2 * weight.size, transcendentals=0
        ),
        name="second_product",
    )(own, other, weight, *parts)


def attention_kernel(
    length_ref, got_ref, keys_ref, values_ref, scale_ref, turn_ref, w_ref, o_ref, w_part_ref, sem
):
    ahead = pltpu.make_async_copy(w_ref.at[pl.ds(0, w_part_ref.shape[0])], w_part_ref, sem)
    ahead.start()
    copies, parts, per_part, _ = o_ref.shape
    heads_of = (got_ref.shape[2] - LANES) // LANES
    group = QUERY_HEADS // KEY_VALUE_HEADS
    sources = group // heads_of
    q_cols = heads_of * LANES
    slots = keys_ref.shape[1]
    inverse_scale = HEAD_SIZE ** (-0.5)
    cosine, sine = turn_ref[0:1], turn_ref[1:2]

    def rounded(w, at, size):
        total = got_ref[2 * w, :, at : at + size] + got_ref[2 * w + 1, :, at : at + size]
        return total.astype(jnp.bfloat16).astype(jnp.float32)

    def rotate(x):
        return x * cosine + pltpu.roll(x, HEAD_SIZE // 2, 1) * sine

    live = lax.broadcasted_iota(jnp.int32, (group, slots), 1) < jnp.concatenate(
        [length_ref[...]] * (slots // LANES), axis=1
    )
    for g in range(KEY_VALUE_HEADS):
        span = slice(g * HEAD_SIZE, (g + 1) * HEAD_SIZE)
        rows = []
        for w in range(g * sources, (g + 1) * sources):
            rows.append(rounded(w, 0, q_cols).reshape(heads_of, LANES))
        rotated = rotate(jnp.concatenate(rows, axis=0))
        fresh_key = rotate(rounded(g, q_cols, LANES)).astype(jnp.bfloat16).astype(jnp.float32)
        fresh_value = rounded(KEY_VALUE_HEADS + g, q_cols, LANES)
        cache_query = (rotated * scale_ref[:, span] * inverse_scale).astype(jnp.bfloat16)
        fresh_query = (rotated * inverse_scale).astype(jnp.bfloat16).astype(jnp.float32)
        scores = lax.dot_general(
            cache_query,
            keys_ref[0, :, span],
            (((1,), (1,)), ((), ())),
            preferred_element_type=jnp.float32,
        )
        fresh_score = jnp.sum(fresh_query * fresh_key, axis=-1, keepdims=True)
        masked = jnp.where(live, scores, jnp.float32(-1e30))
        top = jnp.maximum(jnp.max(masked, axis=-1, keepdims=True), fresh_score)
        exps = jnp.where(live, jnp.exp(masked - top), jnp.float32(0.0))
        fresh_exp = jnp.exp(fresh_score - top)
        total = jnp.sum(exps, axis=-1, keepdims=True) + fresh_exp
        summed = jnp.dot(
            exps.astype(jnp.bfloat16), values_ref[0, :, span], preferred_element_type=jnp.float32
        )
        summed = summed + fresh_exp.astype(jnp.bfloat16).astype(jnp.float32) * fresh_value
        attended = (summed / total).astype(jnp.bfloat16)
        part, at = divmod(g * group, per_part)
        for copy in range(copies):
            o_ref[copy, part, at : at + group, :] = attended
    ahead.wait()


def attention(got, keys, values, scale, lengths, turn, out_weight, ahead, copies, parts):
    out_weight = pltpu.with_memory_space_constraint(out_weight, pltpu.HBM)
    keys = pltpu.with_memory_space_constraint(keys, pltpu.VMEM)
    values = pltpu.with_memory_space_constraint(values, pltpu.VMEM)
    return pl.pallas_call(
        attention_kernel,
        out_shape=(
            jax.ShapeDtypeStruct((copies, parts, QUERY_HEADS // parts, HEAD_SIZE), jnp.bfloat16),
            pltpu.VMEM((ahead, out_weight.shape[1]), out_weight.dtype),
        ),
        in_specs=[WHOLE] * 6 + [pl.BlockSpec(memory_space=pltpu.HBM)],
        out_specs=(WHOLE, WHOLE),
        scratch_shapes=[pltpu.SemaphoreType.DMA],
        compiler_params=params(8),
        cost_estimate=pl.CostEstimate(
            flops=4 * QUERY_HEADS * keys.shape[1] * HEAD_SIZE,
            bytes_accessed=4 * keys.size,
            transcendentals=QUERY_HEADS * keys.shape[1],
        ),
        name="attention",
    )(lengths, got, keys, values, scale, turn, out_weight)


def fits(tokens, q_weight, key_value_weight, stored_keys):
    return (
        lax.axis_size(WIDE) == 16
        and lax.axis_size("narrow") == 2
        and tokens.shape[0] == 2
        and stored_keys.shape[0] == 1
        and q_weight.shape[1] % 1024 == 0
        and key_value_weight.shape[1] == LANES
        and q_weight.shape[0] % 8192 == 0
    )


def tiled_body(
    tokens,
    q_weight,
    key_value_weight,
    out_weight,
    stored_keys,
    stored_values,
    channel_key_scale,
    lengths,
):
    count = lax.axis_size(WIDE)
    narrow = lax.axis_size("narrow")
    eighth = q_weight.shape[0] // 8
    q_parts = []
    held, held_rows = tokens, []
    for step, first, last in ((8, 0, 2), (4, 2, 5), (2, 5, 8)):
        other = lax.ppermute(held, WIDE, [(i, i ^ step) for i in range(count)])
        part = load(q_weight, first * eighth, (last - first) * eighth, *held_rows)
        if held_rows:
            held = join(held, other, part)
        else:
            held, turn, lengths = opening(tokens, other, lengths, part)
        q_parts.append(part)
        held_rows = [held]
    other = lax.ppermute(held, WIDE, [(i, i ^ 1) for i in range(count)])
    kv_part = load(key_value_weight, 0, key_value_weight.shape[0], held)
    partial_terms = first_product(held, other, q_parts, kv_part)
    got = lax.all_to_all(partial_terms, EVERY, split_axis=0, concat_axis=0, tiled=True)
    ahead = 1536
    attended, first_part = attention(
        got,
        stored_keys,
        stored_values,
        channel_key_scale,
        lengths,
        turn,
        out_weight,
        ahead,
        lax.axis_size("hi"),
        narrow,
    )
    mine = lax.all_to_all(
        attended.reshape((-1,) + attended.shape[2:]),
        ("hi", "narrow"),
        split_axis=0,
        concat_axis=0,
        tiled=True,
    )
    other = lax.ppermute(mine, "lo", [(0, 1), (1, 0)])
    second_part = load(out_weight, ahead, 1024, mine)
    keep, send = second_product(mine, other, out_weight, (first_part, second_part))
    return (keep + lax.ppermute(send, "narrow", [(0, 1), (1, 0)])).astype(jnp.bfloat16)


def body(*arguments):
    tokens, q_weight, key_value_weight, _, stored_keys = arguments[:5]
    if fits(tokens, q_weight, key_value_weight, stored_keys):
        return tiled_body(*arguments)
    return general_body(*arguments)


def solution(mesh):
    high, low, narrow = mesh.shape["wide"] // 2, 2, mesh.shape["narrow"]
    fine = Mesh(mesh.devices.reshape(high, low, narrow), EVERY)
    placed = (
        P(WIDE, "narrow"),
        P("narrow", WIDE),
        P("narrow", WIDE),
        P("narrow", WIDE),
        P(EVERY, None, None),
        P(EVERY, None, None),
        P(EVERY, None),
        P(EVERY),
    )
    return jax.shard_map(
        body, mesh=fine, in_specs=placed, out_specs=P("narrow", WIDE), check_vma=False
    )
```

```python
import functools
import math

import jax
import jax.numpy as jnp
from jax import lax
from jax.experimental import pallas as pl
from jax.experimental.pallas import tpu as pltpu
from jax.sharding import Mesh
from jax.sharding import PartitionSpec as P

QUERY_HEADS = 128
KEY_VALUE_HEADS = 8
HEAD_SIZE = 128

WIDE = ("hi", "lo")
EVERY = ("hi", "lo", "narrow")


def apply_rotation(values, token_position):
    half = values.shape[-1] // 2
    freq = jnp.exp(jnp.arange(half, dtype=jnp.float32) * (-2.0 * math.log(500000.0) / HEAD_SIZE))
    angle = token_position * freq
    cosine = jnp.cos(angle)
    sine = jnp.sin(angle)
    first = values[..., :half]
    second = values[..., half:]
    return jnp.concatenate(
        [first * cosine - second * sine, second * cosine + first * sine], axis=-1
    )


def attend(query_vector, current_token, stored_keys, stored_values, channel_key_scale, lengths):
    owning_devices = query_vector.shape[0]
    slot_indices = stored_keys.shape[1]
    group_index = QUERY_HEADS // KEY_VALUE_HEADS
    inverse_scale = HEAD_SIZE ** (-0.5)
    token_position = lengths.astype(jnp.float32)
    rotated_query = apply_rotation(
        query_vector.astype(jnp.float32).reshape(
            owning_devices, KEY_VALUE_HEADS, group_index, HEAD_SIZE
        ),
        token_position[:, None, None, None],
    )
    rotated_key = apply_rotation(
        current_token[:, : KEY_VALUE_HEADS * HEAD_SIZE]
        .astype(jnp.float32)
        .reshape(owning_devices, KEY_VALUE_HEADS, HEAD_SIZE),
        token_position[:, None, None],
    )
    current_value = current_token[:, KEY_VALUE_HEADS * HEAD_SIZE :].reshape(
        owning_devices, KEY_VALUE_HEADS, HEAD_SIZE
    )
    stored_query = (
        rotated_query
        * channel_key_scale.reshape(owning_devices, KEY_VALUE_HEADS, 1, HEAD_SIZE)
        * inverse_scale
    ).astype(jnp.bfloat16)
    fresh_query = (rotated_query * inverse_scale).astype(jnp.bfloat16)
    fresh_key = rotated_key.astype(jnp.bfloat16)
    keys_divided = stored_keys.reshape(owning_devices, slot_indices, KEY_VALUE_HEADS, HEAD_SIZE)
    values_divided = stored_values.reshape(owning_devices, slot_indices, KEY_VALUE_HEADS, HEAD_SIZE)
    scores = jnp.einsum(
        "rgic,rpgc->rgip", stored_query, keys_divided, preferred_element_type=jnp.float32
    )
    fresh_score = jnp.sum(
        fresh_query.astype(jnp.float32) * fresh_key.astype(jnp.float32)[:, :, None, :], axis=-1
    )
    valid = (
        jnp.arange(slot_indices, dtype=jnp.int32)[None, None, None, :]
        < lengths[:, None, None, None]
    )
    masked = jnp.where(valid, scores, jnp.float32(-1e30))
    top = jnp.maximum(jnp.max(masked, axis=-1), fresh_score)
    exps = jnp.where(valid, jnp.exp(masked - top[..., None]), jnp.float32(0.0))
    fresh_exp = jnp.exp(fresh_score - top)
    total = jnp.sum(exps, axis=-1) + fresh_exp
    weights = exps.astype(jnp.bfloat16)
    fresh_weight = fresh_exp.astype(jnp.bfloat16)
    summed = jnp.einsum(
        "rgip,rpgc->rgic", weights, values_divided, preferred_element_type=jnp.float32
    )
    summed = (
        summed
        + fresh_weight.astype(jnp.float32)[..., None]
        * current_value.astype(jnp.float32)[:, :, None, :]
    )
    return (
        (summed / total[..., None])
        .astype(jnp.bfloat16)
        .reshape(owning_devices, QUERY_HEADS * HEAD_SIZE)
    )


def gather_wide(block):
    count = lax.axis_size(WIDE)
    me = lax.axis_index(WIDE)
    held = block
    depth = 0
    step = count // 2
    while step:
        other = lax.ppermute(held, WIDE, [(i, i ^ step) for i in range(count)])
        upper = (me & step) != 0
        held = jnp.stack(
            [jnp.where(upper, other, held), jnp.where(upper, held, other)], axis=depth
        )
        depth += 1
        step //= 2
    return held.reshape((count * block.shape[0],) + block.shape[1:])


def general_body(
    tokens,
    q_weight,
    key_value_weight,
    out_weight,
    stored_keys,
    stored_values,
    channel_key_scale,
    lengths,
):
    high = lax.axis_size("hi")
    low = lax.axis_size("lo")
    wide_count = high * low
    narrow = lax.axis_size("narrow")
    query_cols = q_weight.shape[1]
    row_width = query_cols + key_value_weight.shape[1]
    per_owner = stored_keys.shape[0]
    piece = gather_wide(tokens)
    partial_terms = jnp.concatenate(
        [
            jnp.dot(piece, q_weight, preferred_element_type=jnp.float32),
            jnp.dot(piece, key_value_weight, preferred_element_type=jnp.float32),
        ],
        axis=1,
    )
    received = lax.all_to_all(partial_terms, EVERY, split_axis=0, concat_axis=0, tiled=True)
    received = received.reshape(wide_count, narrow, per_owner, row_width)
    owned = jnp.sum(received, axis=1).astype(jnp.bfloat16).transpose(1, 0, 2)
    query_vector = owned[:, :, :query_cols].reshape(per_owner, wide_count * query_cols)
    current_token = owned[:, :, query_cols:].reshape(
        per_owner, wide_count * (row_width - query_cols)
    )
    attended = attend(
        query_vector, current_token, stored_keys, stored_values, channel_key_scale, lengths
    )
    depth = out_weight.shape[0]
    parts = attended.reshape(per_owner, narrow, depth).transpose(1, 0, 2)
    parts = jnp.broadcast_to(parts[None], (high, narrow, per_owner, depth))
    mine = lax.all_to_all(
        parts.reshape(high * narrow * per_owner, depth),
        ("hi", "narrow"),
        split_axis=0,
        concat_axis=0,
        tiled=True,
    ).reshape(high, 1, narrow * per_owner, depth)
    ordered = lax.all_gather(mine, "lo", axis=1, tiled=True)
    ordered = ordered.reshape(wide_count * narrow * per_owner, depth)
    terms = jnp.dot(ordered, out_weight, preferred_element_type=jnp.float32)
    return sum_narrow(terms).astype(jnp.bfloat16)


def sum_narrow(terms):
    narrow = lax.axis_size("narrow")
    me = lax.axis_index("narrow")
    rows = terms.shape[0] // narrow
    grouped = terms.reshape(narrow, rows, terms.shape[1])
    total = lax.dynamic_index_in_dim(grouped, me, 0, keepdims=False)
    for step in range(1, narrow):
        target = lax.rem(me + step, narrow)
        leaving = lax.dynamic_index_in_dim(grouped, target, 0, keepdims=False)
        total = total + lax.ppermute(
            leaving, "narrow", [(i, (i + step) % narrow) for i in range(narrow)]
        )
    return total


WHOLE = pl.BlockSpec(memory_space=pltpu.VMEM)
LANES = 128


def params(mebibytes):
    return pltpu.CompilerParams(vmem_limit_bytes=mebibytes << 20)


def join_kernel(a_ref, b_ref, _, o_ref):
    rows = a_ref.shape[0]
    o_ref[:rows] = a_ref[...]
    o_ref[rows:] = b_ref[...]


def join(a, b, ready):
    ready = pltpu.with_memory_space_constraint(ready, pltpu.VMEM)
    return pl.pallas_call(
        join_kernel,
        out_shape=jax.ShapeDtypeStruct((2 * a.shape[0],) + a.shape[1:], a.dtype),
        in_specs=[WHOLE] * 3,
        out_specs=WHOLE,
        compiler_params=params(2),
        cost_estimate=pl.CostEstimate(flops=0, bytes_accessed=8 * a.size, transcendentals=0),
        name="join_rows",
    )(a, b, ready)


def place_rows(piece_ref, turned, block, first, blocks):
    tiles = piece_ref.shape[1]
    for j in range(piece_ref.shape[0] // block):
        at = pl.multiple_of(blocks(j) * (block * tiles), block * tiles)
        turned[pl.ds(at, block * tiles), :] = (
            piece_ref[j * block : (j + 1) * block].reshape(block * tiles, LANES).astype(jnp.float32)
        )


def turned_rows(turned, rows, tiles, first, count):
    return jnp.concatenate(
        [turned[pl.ds(first + t, rows, stride=tiles), :] for t in range(count)], axis=1
    ).astype(jnp.bfloat16)


def as_tiles(row, tiles):
    return jnp.concatenate(
        [row[:, t * LANES : (t + 1) * LANES] for t in range(tiles)], axis=0
    ).astype(jnp.bfloat16)


def opening_kernel(own_ref, other_ref, length_ref, _, rows_ref, turn_ref, length_row_ref):
    _, tiles, _ = rows_ref.shape
    rows = own_ref.shape[0]
    for i, ref in enumerate((own_ref, other_ref)):
        values = ref[...].astype(jnp.float32)
        for r in range(rows):
            rows_ref[i * rows + r] = as_tiles(values[r : r + 1], tiles)
    half = HEAD_SIZE // 2
    lane = lax.broadcasted_iota(jnp.int32, (1, HEAD_SIZE), 1)
    index = jnp.where(lane < half, lane, lane - half).astype(jnp.float32)
    freq = jnp.exp(index * (-2.0 * math.log(500000.0) / HEAD_SIZE))
    length = jnp.full((1, HEAD_SIZE), length_ref[0], jnp.int32)
    angle = length.astype(jnp.float32) * freq
    sine = jnp.sin(angle)
    turn_ref[0:1] = jnp.cos(angle)
    turn_ref[1:2] = jnp.where(lane < half, -sine, sine)
    length_row_ref[...] = length


def opening(tokens, other, lengths, ready):
    rows, width = tokens.shape
    ready = pltpu.with_memory_space_constraint(ready, pltpu.VMEM)
    return pl.pallas_call(
        opening_kernel,
        out_shape=(
            jax.ShapeDtypeStruct((2 * rows, width // LANES, LANES), tokens.dtype),
            jax.ShapeDtypeStruct((2, HEAD_SIZE), jnp.float32),
            jax.ShapeDtypeStruct((1, HEAD_SIZE), jnp.int32),
        ),
        in_specs=[WHOLE, WHOLE, pl.BlockSpec(memory_space=pltpu.SMEM), WHOLE],
        out_specs=(WHOLE,) * 3,
        compiler_params=params(2),
        cost_estimate=pl.CostEstimate(flops=0, bytes_accessed=8 * tokens.size, transcendentals=0),
        name="opening",
    )(tokens, other, lengths, ready)


def load_kernel(first, weight_ref, *refs):
    *_, o_ref, sem = refs
    rows = o_ref.shape[0]
    copy = pltpu.make_async_copy(weight_ref.at[pl.ds(first, rows)], o_ref, sem)
    copy.start()
    copy.wait()


def load(weight, first, rows, *after):
    weight = pltpu.with_memory_space_constraint(weight, pltpu.HBM)
    return pl.pallas_call(
        functools.partial(load_kernel, first),
        out_shape=pltpu.VMEM((rows, weight.shape[1]), weight.dtype),
        in_specs=[pl.BlockSpec(memory_space=pltpu.HBM)]
        + [pl.BlockSpec(memory_space=pl.ANY)] * len(after),
        out_specs=WHOLE,
        scratch_shapes=[pltpu.SemaphoreType.DMA],
        compiler_params=params(1),
        cost_estimate=pl.CostEstimate(
            flops=0, bytes_accessed=2 * rows * weight.shape[1], transcendentals=0
        ),
        name="load",
    )(weight, *after)


def first_product_kernel(own_ref, other_ref, w_ref, *refs):
    *q_refs, kv_ref, o_ref, w_part_ref, turned, sem = refs
    ahead = pltpu.make_async_copy(w_ref.at[pl.ds(0, w_part_ref.shape[0])], w_part_ref, sem)
    ahead.start()
    me = lax.axis_index(WIDE)
    pair = 2
    rows = 2 * own_ref.shape[0]
    tiles = own_ref.shape[1]
    count = rows // pair
    bits = count.bit_length() - 1

    def source(j, last):
        mask = last
        for bit in range(bits - 1):
            if j >> bit & 1:
                mask |= count >> (bit + 1)
        return me ^ mask

    place_rows(own_ref, turned, pair, 0, lambda j: source(j, 0))
    place_rows(other_ref, turned, pair, 0, lambda j: source(j, 1))
    group = 8
    deep = group * LANES
    q_cols, kv_cols = q_refs[0].shape[1], kv_ref.shape[1]
    totals = jnp.zeros((rows, q_cols), jnp.float32), jnp.zeros((rows, kv_cols), jnp.float32)
    base = 0
    for q_ref in q_refs:

        def step(k, carry):
            q_total, kv_total = carry
            x = turned_rows(turned, rows, tiles, (base // LANES) + k * group, group)
            at = pl.multiple_of(k * deep, deep)
            q_total = q_total + jnp.dot(
                x, q_ref[pl.ds(at, deep), :], preferred_element_type=jnp.float32
            )
            kv_total = kv_total + jnp.dot(
                x, kv_ref[pl.ds(base + at, deep), :], preferred_element_type=jnp.float32
            )
            return q_total, kv_total

        totals = lax.fori_loop(0, q_ref.shape[0] // deep, step, totals)
        base += q_ref.shape[0]
    q_total, kv_total = totals
    for r in range(rows):
        o_ref[r, :, :q_cols] = q_total[r : r + 1]
        o_ref[r, :, q_cols:] = kv_total[r : r + 1]
    ahead.wait()


def first_product(own, other, q_parts, kv_weight, out_weight, ahead):
    out_weight = pltpu.with_memory_space_constraint(out_weight, pltpu.HBM)
    rows = 2 * own.shape[0]
    depth = kv_weight.shape[0]
    width = q_parts[0].shape[1] + kv_weight.shape[1]
    weights = [pltpu.with_memory_space_constraint(w, pltpu.VMEM) for w in (*q_parts, kv_weight)]
    return pl.pallas_call(
        first_product_kernel,
        out_shape=(
            jax.ShapeDtypeStruct((rows, 1, width), jnp.float32),
            pltpu.VMEM((ahead, out_weight.shape[1]), out_weight.dtype),
        ),
        in_specs=[WHOLE, WHOLE, pl.BlockSpec(memory_space=pltpu.HBM)] + [WHOLE] * len(weights),
        out_specs=(WHOLE, WHOLE),
        scratch_shapes=[
            pltpu.VMEM((rows * own.shape[1], LANES), jnp.float32),
            pltpu.SemaphoreType.DMA,
        ],
        compiler_params=params(6),
        cost_estimate=pl.CostEstimate(
            flops=2 * rows * depth * width,
            bytes_accessed=4 * own.size + 2 * depth * width,
            transcendentals=0,
        ),
        name="first_product",
    )(own, other, out_weight, *weights)


def second_product_kernel(own_ref, other_ref, w_ref, *refs):
    *parts, keep_ref, send_ref, turned, w_buf, sems = refs
    low = lax.axis_index("lo")
    mine = lax.axis_index("narrow")
    chunks = w_buf.shape[0]
    deep = w_buf.shape[1]
    base = sum(part.shape[0] for part in parts)
    copies = [
        pltpu.make_async_copy(w_ref.at[pl.ds(base + c * deep, deep)], w_buf.at[c], sems.at[c])
        for c in range(chunks)
    ]
    for copy in copies:
        copy.start()
    pair = 2
    rows = 2 * own_ref.shape[0]
    tiles = own_ref.shape[1]
    place_rows(own_ref, turned, pair, 0, lambda j: 2 * j + low)
    place_rows(other_ref, turned, pair, 0, lambda j: 2 * j + (1 - low))
    total = jnp.zeros((rows, w_ref.shape[1]), jnp.float32)
    at = 0
    for part in parts:
        x = turned_rows(turned, rows, tiles, at // LANES, part.shape[0] // LANES)
        total = total + jnp.dot(x, part[...], preferred_element_type=jnp.float32)
        at += part.shape[0]
    for c in range(chunks):
        x = turned_rows(turned, rows, tiles, (at + c * deep) // LANES, deep // LANES)
        copies[c].wait()
        total = total + jnp.dot(x, w_buf[c], preferred_element_type=jnp.float32)
    half = rows // 2
    lower = mine == 0
    keep_ref[...] = jnp.where(lower, total[:half], total[half:])
    send_ref[...] = jnp.where(lower, total[half:], total[:half])


def second_product(own, other, weight, parts):
    rows = 2 * own.shape[0]
    cols = weight.shape[1]
    deep = 512
    chunks = (weight.shape[0] - sum(part.shape[0] for part in parts)) // deep
    weight = pltpu.with_memory_space_constraint(weight, pltpu.HBM)
    parts = [pltpu.with_memory_space_constraint(part, pltpu.VMEM) for part in parts]
    half = jax.ShapeDtypeStruct((rows // 2, cols), jnp.float32)
    return pl.pallas_call(
        second_product_kernel,
        out_shape=(half, half),
        in_specs=[WHOLE, WHOLE, pl.BlockSpec(memory_space=pltpu.HBM)] + [WHOLE] * len(parts),
        out_specs=(WHOLE, WHOLE),
        scratch_shapes=[
            pltpu.VMEM((rows * own.shape[1], LANES), jnp.float32),
            pltpu.VMEM((chunks, deep, cols), weight.dtype),
            pltpu.SemaphoreType.DMA((chunks,)),
        ],
        compiler_params=params(24),
        cost_estimate=pl.CostEstimate(
            flops=2 * rows * weight.size, bytes_accessed=4 * own.size + 2 * weight.size, transcendentals=0
        ),
        name="second_product",
    )(own, other, weight, *parts)


def attention_kernel(
    first,
    length_ref,
    got_ref,
    keys_ref,
    values_ref,
    scale_ref,
    turn_ref,
    w_ref,
    o_ref,
    w_part_ref,
    sem,
):
    ahead = pltpu.make_async_copy(w_ref.at[pl.ds(first, w_part_ref.shape[0])], w_part_ref, sem)
    ahead.start()
    copies, parts, per_part, _ = o_ref.shape
    heads_of = (got_ref.shape[2] - LANES) // LANES
    group = QUERY_HEADS // KEY_VALUE_HEADS
    sources = group // heads_of
    q_cols = heads_of * LANES
    slots = keys_ref.shape[1]
    inverse_scale = HEAD_SIZE ** (-0.5)
    cosine, sine = turn_ref[0:1], turn_ref[1:2]

    def rounded(w, at, size):
        total = got_ref[2 * w, :, at : at + size] + got_ref[2 * w + 1, :, at : at + size]
        return total.astype(jnp.bfloat16).astype(jnp.float32)

    def rotate(x):
        return x * cosine + pltpu.roll(x, HEAD_SIZE // 2, 1) * sine

    live = lax.broadcasted_iota(jnp.int32, (2 * group, slots), 1) < jnp.concatenate(
        [length_ref[...]] * (slots // LANES), axis=1
    )
    none = jnp.zeros((group, HEAD_SIZE), jnp.bfloat16)
    pairs = range(0, KEY_VALUE_HEADS, 2)
    scored = []
    for pair in pairs:
        cache, fresh, fresh_values = [], [], []
        for g in (pair, pair + 1):
            rows = [
                rounded(w, 0, q_cols).reshape(heads_of, LANES)
                for w in range(g * sources, (g + 1) * sources)
            ]
            rotated = rotate(jnp.concatenate(rows, axis=0))
            fresh_key = rotate(rounded(g, q_cols, LANES)).astype(jnp.bfloat16).astype(jnp.float32)
            scale = scale_ref[:, g * HEAD_SIZE : (g + 1) * HEAD_SIZE]
            cache.append((rotated * scale * inverse_scale).astype(jnp.bfloat16))
            fresh_query = (rotated * inverse_scale).astype(jnp.bfloat16).astype(jnp.float32)
            fresh.append(jnp.sum(fresh_query * fresh_key, axis=-1, keepdims=True))
            fresh_values.append(
                jnp.broadcast_to(rounded(KEY_VALUE_HEADS + g, q_cols, LANES), (group, HEAD_SIZE))
            )
        queries = jnp.concatenate(
            [
                jnp.concatenate([cache[0], none], axis=1),
                jnp.concatenate([none, cache[1]], axis=1),
            ],
            axis=0,
        )
        span = slice(pair * HEAD_SIZE, (pair + 2) * HEAD_SIZE)
        scores = lax.dot_general(
            queries,
            keys_ref[0, :, span],
            (((1,), (1,)), ((), ())),
            preferred_element_type=jnp.float32,
        )
        scored.append((scores, jnp.concatenate(fresh, axis=0), fresh_values))
    for pair, (scores, fresh_score, fresh_values) in zip(pairs, scored, strict=True):
        masked = jnp.where(live, scores, jnp.float32(-1e30))
        top = jnp.maximum(jnp.max(masked, axis=-1, keepdims=True), fresh_score)
        exps = jnp.where(live, jnp.exp(masked - top), jnp.float32(0.0))
        fresh_exp = jnp.exp(fresh_score - top)
        total = jnp.sum(exps, axis=-1, keepdims=True) + fresh_exp
        span = slice(pair * HEAD_SIZE, (pair + 2) * HEAD_SIZE)
        both = jnp.dot(
            exps.astype(jnp.bfloat16), values_ref[0, :, span], preferred_element_type=jnp.float32
        )
        summed = jnp.concatenate([both[:group, :HEAD_SIZE], both[group:, HEAD_SIZE:]], axis=0)
        fresh_weight = fresh_exp.astype(jnp.bfloat16).astype(jnp.float32)
        summed = summed + fresh_weight * jnp.concatenate(fresh_values, axis=0)
        attended = (summed / total).astype(jnp.bfloat16)
        part, at = divmod(pair * group, per_part)
        for copy in range(copies):
            o_ref[copy, part, at : at + 2 * group, :] = attended
    ahead.wait()


def attention(
    got, keys, values, scale, lengths, turn, out_weight, first, ahead, copies, parts
):
    out_weight = pltpu.with_memory_space_constraint(out_weight, pltpu.HBM)
    keys = pltpu.with_memory_space_constraint(keys, pltpu.VMEM)
    values = pltpu.with_memory_space_constraint(values, pltpu.VMEM)
    return pl.pallas_call(
        functools.partial(attention_kernel, first),
        out_shape=(
            jax.ShapeDtypeStruct((copies, parts, QUERY_HEADS // parts, HEAD_SIZE), jnp.bfloat16),
            pltpu.VMEM((ahead, out_weight.shape[1]), out_weight.dtype),
        ),
        in_specs=[WHOLE] * 6 + [pl.BlockSpec(memory_space=pltpu.HBM)],
        out_specs=(WHOLE, WHOLE),
        scratch_shapes=[pltpu.SemaphoreType.DMA],
        compiler_params=params(8),
        cost_estimate=pl.CostEstimate(
            flops=4 * QUERY_HEADS * keys.shape[1] * HEAD_SIZE,
            bytes_accessed=4 * keys.size,
            transcendentals=QUERY_HEADS * keys.shape[1],
        ),
        name="attention",
    )(lengths, got, keys, values, scale, turn, out_weight)


def fits(tokens, q_weight, key_value_weight, stored_keys):
    return (
        lax.axis_size(WIDE) == 16
        and lax.axis_size("narrow") == 2
        and tokens.shape[0] == 2
        and stored_keys.shape[0] == 1
        and q_weight.shape[1] % 1024 == 0
        and key_value_weight.shape[1] == LANES
        and q_weight.shape[0] % 8192 == 0
    )


def tiled_body(
    tokens,
    q_weight,
    key_value_weight,
    out_weight,
    stored_keys,
    stored_values,
    channel_key_scale,
    lengths,
):
    count = lax.axis_size(WIDE)
    narrow = lax.axis_size("narrow")
    eighth = q_weight.shape[0] // 8
    q_parts = []
    held, held_rows = tokens, []
    for step, first, last in ((8, 0, 2), (4, 2, 5), (2, 5, 8)):
        other = lax.ppermute(held, WIDE, [(i, i ^ step) for i in range(count)])
        part = load(q_weight, first * eighth, (last - first) * eighth, *held_rows)
        if held_rows:
            held = join(held, other, part)
        else:
            held, turn, lengths = opening(tokens, other, lengths, part)
        q_parts.append(part)
        held_rows = [held]
    other = lax.ppermute(held, WIDE, [(i, i ^ 1) for i in range(count)])
    kv_part = load(key_value_weight, 0, key_value_weight.shape[0], held)
    ahead, next_rows, last_rows = 1280, 256, 1024
    partial_terms, first_part = first_product(held, other, q_parts, kv_part, out_weight, ahead)
    got = lax.all_to_all(partial_terms, EVERY, split_axis=0, concat_axis=0, tiled=True)
    attended, next_part = attention(
        got,
        stored_keys,
        stored_values,
        channel_key_scale,
        lengths,
        turn,
        out_weight,
        ahead,
        next_rows,
        lax.axis_size("hi"),
        narrow,
    )
    mine = lax.all_to_all(
        attended.reshape((-1,) + attended.shape[2:]),
        ("hi", "narrow"),
        split_axis=0,
        concat_axis=0,
        tiled=True,
    )
    other = lax.ppermute(mine, "lo", [(0, 1), (1, 0)])
    last_part = load(out_weight, ahead + next_rows, last_rows, mine)
    keep, send = second_product(mine, other, out_weight, (first_part, next_part, last_part))
    return (keep + lax.ppermute(send, "narrow", [(0, 1), (1, 0)])).astype(jnp.bfloat16)


def body(*arguments):
    tokens, q_weight, key_value_weight, _, stored_keys = arguments[:5]
    if fits(tokens, q_weight, key_value_weight, stored_keys):
        return tiled_body(*arguments)
    return general_body(*arguments)


def solution(mesh):
    high, low, narrow = mesh.shape["wide"] // 2, 2, mesh.shape["narrow"]
    fine = Mesh(mesh.devices.reshape(high, low, narrow), EVERY)
    placed = (
        P(WIDE, "narrow"),
        P("narrow", WIDE),
        P("narrow", WIDE),
        P("narrow", WIDE),
        P(EVERY, None, None),
        P(EVERY, None, None),
        P(EVERY, None),
        P(EVERY),
    )
    return jax.shard_map(
        body, mesh=fine, in_specs=placed, out_specs=P("narrow", WIDE), check_vma=False
    )
```

```python
import functools
import math

import jax
import jax.numpy as jnp
from jax import lax
from jax.experimental import pallas as pl
from jax.experimental.pallas import tpu as pltpu
from jax.sharding import Mesh
from jax.sharding import PartitionSpec as P

QUERY_HEADS = 128
KEY_VALUE_HEADS = 8
HEAD_SIZE = 128

WIDE = ("hi", "lo")
EVERY = ("hi", "lo", "narrow")


def apply_rotation(values, token_position):
    half = values.shape[-1] // 2
    freq = jnp.exp(jnp.arange(half, dtype=jnp.float32) * (-2.0 * math.log(500000.0) / HEAD_SIZE))
    angle = token_position * freq
    cosine = jnp.cos(angle)
    sine = jnp.sin(angle)
    first = values[..., :half]
    second = values[..., half:]
    return jnp.concatenate(
        [first * cosine - second * sine, second * cosine + first * sine], axis=-1
    )


def attend(query_vector, current_token, stored_keys, stored_values, channel_key_scale, lengths):
    owning_devices = query_vector.shape[0]
    slot_indices = stored_keys.shape[1]
    group_index = QUERY_HEADS // KEY_VALUE_HEADS
    inverse_scale = HEAD_SIZE ** (-0.5)
    token_position = lengths.astype(jnp.float32)
    rotated_query = apply_rotation(
        query_vector.astype(jnp.float32).reshape(
            owning_devices, KEY_VALUE_HEADS, group_index, HEAD_SIZE
        ),
        token_position[:, None, None, None],
    )
    rotated_key = apply_rotation(
        current_token[:, : KEY_VALUE_HEADS * HEAD_SIZE]
        .astype(jnp.float32)
        .reshape(owning_devices, KEY_VALUE_HEADS, HEAD_SIZE),
        token_position[:, None, None],
    )
    current_value = current_token[:, KEY_VALUE_HEADS * HEAD_SIZE :].reshape(
        owning_devices, KEY_VALUE_HEADS, HEAD_SIZE
    )
    stored_query = (
        rotated_query
        * channel_key_scale.reshape(owning_devices, KEY_VALUE_HEADS, 1, HEAD_SIZE)
        * inverse_scale
    ).astype(jnp.bfloat16)
    fresh_query = (rotated_query * inverse_scale).astype(jnp.bfloat16)
    fresh_key = rotated_key.astype(jnp.bfloat16)
    keys_divided = stored_keys.reshape(owning_devices, slot_indices, KEY_VALUE_HEADS, HEAD_SIZE)
    values_divided = stored_values.reshape(owning_devices, slot_indices, KEY_VALUE_HEADS, HEAD_SIZE)
    scores = jnp.einsum(
        "rgic,rpgc->rgip", stored_query, keys_divided, preferred_element_type=jnp.float32
    )
    fresh_score = jnp.sum(
        fresh_query.astype(jnp.float32) * fresh_key.astype(jnp.float32)[:, :, None, :], axis=-1
    )
    valid = (
        jnp.arange(slot_indices, dtype=jnp.int32)[None, None, None, :]
        < lengths[:, None, None, None]
    )
    masked = jnp.where(valid, scores, jnp.float32(-1e30))
    top = jnp.maximum(jnp.max(masked, axis=-1), fresh_score)
    exps = jnp.where(valid, jnp.exp(masked - top[..., None]), jnp.float32(0.0))
    fresh_exp = jnp.exp(fresh_score - top)
    total = jnp.sum(exps, axis=-1) + fresh_exp
    weights = exps.astype(jnp.bfloat16)
    fresh_weight = fresh_exp.astype(jnp.bfloat16)
    summed = jnp.einsum(
        "rgip,rpgc->rgic", weights, values_divided, preferred_element_type=jnp.float32
    )
    summed = (
        summed
        + fresh_weight.astype(jnp.float32)[..., None]
        * current_value.astype(jnp.float32)[:, :, None, :]
    )
    return (
        (summed / total[..., None])
        .astype(jnp.bfloat16)
        .reshape(owning_devices, QUERY_HEADS * HEAD_SIZE)
    )


def gather_wide(block):
    count = lax.axis_size(WIDE)
    me = lax.axis_index(WIDE)
    held = block
    depth = 0
    step = count // 2
    while step:
        other = lax.ppermute(held, WIDE, [(i, i ^ step) for i in range(count)])
        upper = (me & step) != 0
        held = jnp.stack(
            [jnp.where(upper, other, held), jnp.where(upper, held, other)], axis=depth
        )
        depth += 1
        step //= 2
    return held.reshape((count * block.shape[0],) + block.shape[1:])


def general_body(
    tokens,
    q_weight,
    key_value_weight,
    out_weight,
    stored_keys,
    stored_values,
    channel_key_scale,
    lengths,
):
    high = lax.axis_size("hi")
    low = lax.axis_size("lo")
    wide_count = high * low
    narrow = lax.axis_size("narrow")
    query_cols = q_weight.shape[1]
    row_width = query_cols + key_value_weight.shape[1]
    per_owner = stored_keys.shape[0]
    piece = gather_wide(tokens)
    partial_terms = jnp.concatenate(
        [
            jnp.dot(piece, q_weight, preferred_element_type=jnp.float32),
            jnp.dot(piece, key_value_weight, preferred_element_type=jnp.float32),
        ],
        axis=1,
    )
    received = lax.all_to_all(partial_terms, EVERY, split_axis=0, concat_axis=0, tiled=True)
    received = received.reshape(wide_count, narrow, per_owner, row_width)
    owned = jnp.sum(received, axis=1).astype(jnp.bfloat16).transpose(1, 0, 2)
    query_vector = owned[:, :, :query_cols].reshape(per_owner, wide_count * query_cols)
    current_token = owned[:, :, query_cols:].reshape(
        per_owner, wide_count * (row_width - query_cols)
    )
    attended = attend(
        query_vector, current_token, stored_keys, stored_values, channel_key_scale, lengths
    )
    depth = out_weight.shape[0]
    parts = attended.reshape(per_owner, narrow, depth).transpose(1, 0, 2)
    parts = jnp.broadcast_to(parts[None], (high, narrow, per_owner, depth))
    mine = lax.all_to_all(
        parts.reshape(high * narrow * per_owner, depth),
        ("hi", "narrow"),
        split_axis=0,
        concat_axis=0,
        tiled=True,
    ).reshape(high, 1, narrow * per_owner, depth)
    ordered = lax.all_gather(mine, "lo", axis=1, tiled=True)
    ordered = ordered.reshape(wide_count * narrow * per_owner, depth)
    terms = jnp.dot(ordered, out_weight, preferred_element_type=jnp.float32)
    return sum_narrow(terms).astype(jnp.bfloat16)


def sum_narrow(terms):
    narrow = lax.axis_size("narrow")
    me = lax.axis_index("narrow")
    rows = terms.shape[0] // narrow
    grouped = terms.reshape(narrow, rows, terms.shape[1])
    total = lax.dynamic_index_in_dim(grouped, me, 0, keepdims=False)
    for step in range(1, narrow):
        target = lax.rem(me + step, narrow)
        leaving = lax.dynamic_index_in_dim(grouped, target, 0, keepdims=False)
        total = total + lax.ppermute(
            leaving, "narrow", [(i, (i + step) % narrow) for i in range(narrow)]
        )
    return total


WHOLE = pl.BlockSpec(memory_space=pltpu.VMEM)
LANES = 128


def params(mebibytes):
    return pltpu.CompilerParams(vmem_limit_bytes=mebibytes << 20)


def join_kernel(a_ref, b_ref, _, o_ref):
    rows = a_ref.shape[0]
    o_ref[:rows] = a_ref[...]
    o_ref[rows:] = b_ref[...]


def join(a, b, ready):
    ready = pltpu.with_memory_space_constraint(ready, pltpu.VMEM)
    return pl.pallas_call(
        join_kernel,
        out_shape=jax.ShapeDtypeStruct((2 * a.shape[0],) + a.shape[1:], a.dtype),
        in_specs=[WHOLE] * 3,
        out_specs=WHOLE,
        compiler_params=params(2),
        cost_estimate=pl.CostEstimate(flops=0, bytes_accessed=8 * a.size, transcendentals=0),
        name="join_rows",
    )(a, b, ready)


def place_rows(piece_ref, turned, block, first, blocks):
    tiles = piece_ref.shape[1]
    for j in range(piece_ref.shape[0] // block):
        at = pl.multiple_of(blocks(j) * (block * tiles), block * tiles)
        turned[pl.ds(at, block * tiles), :] = (
            piece_ref[j * block : (j + 1) * block].reshape(block * tiles, LANES).astype(jnp.float32)
        )


def turned_rows(turned, rows, tiles, first, count):
    return jnp.concatenate(
        [turned[pl.ds(first + t, rows, stride=tiles), :] for t in range(count)], axis=1
    ).astype(jnp.bfloat16)


def as_tiles(row, tiles):
    return jnp.concatenate(
        [row[:, t * LANES : (t + 1) * LANES] for t in range(tiles)], axis=0
    ).astype(jnp.bfloat16)


def opening_kernel(own_ref, other_ref, length_ref, _, rows_ref, turn_ref, length_row_ref):
    _, tiles, _ = rows_ref.shape
    rows = own_ref.shape[0]
    for i, ref in enumerate((own_ref, other_ref)):
        values = ref[...].astype(jnp.float32)
        for r in range(rows):
            rows_ref[i * rows + r] = as_tiles(values[r : r + 1], tiles)
    half = HEAD_SIZE // 2
    lane = lax.broadcasted_iota(jnp.int32, (1, HEAD_SIZE), 1)
    index = jnp.where(lane < half, lane, lane - half).astype(jnp.float32)
    freq = jnp.exp(index * (-2.0 * math.log(500000.0) / HEAD_SIZE))
    length = jnp.full((1, HEAD_SIZE), length_ref[0], jnp.int32)
    angle = length.astype(jnp.float32) * freq
    sine = jnp.sin(angle)
    turn_ref[0:1] = jnp.cos(angle)
    turn_ref[1:2] = jnp.where(lane < half, -sine, sine)
    length_row_ref[...] = length


def opening(tokens, other, lengths, ready):
    rows, width = tokens.shape
    ready = pltpu.with_memory_space_constraint(ready, pltpu.VMEM)
    return pl.pallas_call(
        opening_kernel,
        out_shape=(
            jax.ShapeDtypeStruct((2 * rows, width // LANES, LANES), tokens.dtype),
            jax.ShapeDtypeStruct((2, HEAD_SIZE), jnp.float32),
            jax.ShapeDtypeStruct((1, HEAD_SIZE), jnp.int32),
        ),
        in_specs=[WHOLE, WHOLE, pl.BlockSpec(memory_space=pltpu.SMEM), WHOLE],
        out_specs=(WHOLE,) * 3,
        compiler_params=params(2),
        cost_estimate=pl.CostEstimate(flops=0, bytes_accessed=8 * tokens.size, transcendentals=0),
        name="opening",
    )(tokens, other, lengths, ready)


def load_kernel(first, weight_ref, *refs):
    *_, o_ref, sem = refs
    rows = o_ref.shape[0]
    copy = pltpu.make_async_copy(weight_ref.at[pl.ds(first, rows)], o_ref, sem)
    copy.start()
    copy.wait()


def load(weight, first, rows, *after):
    weight = pltpu.with_memory_space_constraint(weight, pltpu.HBM)
    return pl.pallas_call(
        functools.partial(load_kernel, first),
        out_shape=pltpu.VMEM((rows, weight.shape[1]), weight.dtype),
        in_specs=[pl.BlockSpec(memory_space=pltpu.HBM)]
        + [pl.BlockSpec(memory_space=pl.ANY)] * len(after),
        out_specs=WHOLE,
        scratch_shapes=[pltpu.SemaphoreType.DMA],
        compiler_params=params(1),
        cost_estimate=pl.CostEstimate(
            flops=0, bytes_accessed=2 * rows * weight.shape[1], transcendentals=0
        ),
        name="load",
    )(weight, *after)


def first_product_kernel(own_ref, other_ref, w_ref, *refs):
    *q_refs, kv_ref, o_ref, w_part_ref, turned, sem = refs
    ahead = pltpu.make_async_copy(w_ref.at[pl.ds(0, w_part_ref.shape[0])], w_part_ref, sem)
    ahead.start()
    me = lax.axis_index(WIDE)
    pair = 2
    rows = 2 * own_ref.shape[0]
    tiles = own_ref.shape[1]
    count = rows // pair
    bits = count.bit_length() - 1

    def source(j, last):
        mask = last
        for bit in range(bits - 1):
            if j >> bit & 1:
                mask |= count >> (bit + 1)
        return me ^ mask

    place_rows(own_ref, turned, pair, 0, lambda j: source(j, 0))
    place_rows(other_ref, turned, pair, 0, lambda j: source(j, 1))
    group = 8
    deep = group * LANES
    q_cols, kv_cols = q_refs[0].shape[1], kv_ref.shape[1]
    totals = jnp.zeros((rows, q_cols), jnp.float32), jnp.zeros((rows, kv_cols), jnp.float32)
    base = 0
    for q_ref in q_refs:

        def step(k, carry):
            q_total, kv_total = carry
            x = turned_rows(turned, rows, tiles, (base // LANES) + k * group, group)
            at = pl.multiple_of(k * deep, deep)
            q_total = q_total + jnp.dot(
                x, q_ref[pl.ds(at, deep), :], preferred_element_type=jnp.float32
            )
            kv_total = kv_total + jnp.dot(
                x, kv_ref[pl.ds(base + at, deep), :], preferred_element_type=jnp.float32
            )
            return q_total, kv_total

        totals = lax.fori_loop(0, q_ref.shape[0] // deep, step, totals)
        base += q_ref.shape[0]
    q_total, kv_total = totals
    for r in range(rows):
        o_ref[r, :, :q_cols] = q_total[r : r + 1]
        o_ref[r, :, q_cols:] = kv_total[r : r + 1]
    ahead.wait()


def first_product(own, other, q_parts, kv_weight, out_weight, ahead):
    out_weight = pltpu.with_memory_space_constraint(out_weight, pltpu.HBM)
    rows = 2 * own.shape[0]
    depth = kv_weight.shape[0]
    width = q_parts[0].shape[1] + kv_weight.shape[1]
    weights = [pltpu.with_memory_space_constraint(w, pltpu.VMEM) for w in (*q_parts, kv_weight)]
    return pl.pallas_call(
        first_product_kernel,
        out_shape=(
            jax.ShapeDtypeStruct((rows, 1, width), jnp.float32),
            pltpu.VMEM((ahead, out_weight.shape[1]), out_weight.dtype),
        ),
        in_specs=[WHOLE, WHOLE, pl.BlockSpec(memory_space=pltpu.HBM)] + [WHOLE] * len(weights),
        out_specs=(WHOLE, WHOLE),
        scratch_shapes=[
            pltpu.VMEM((rows * own.shape[1], LANES), jnp.float32),
            pltpu.SemaphoreType.DMA,
        ],
        compiler_params=params(6),
        cost_estimate=pl.CostEstimate(
            flops=2 * rows * depth * width,
            bytes_accessed=4 * own.size + 2 * depth * width,
            transcendentals=0,
        ),
        name="first_product",
    )(own, other, out_weight, *weights)


def second_product_kernel(own_ref, other_ref, w_ref, *refs):
    *parts, keep_ref, send_ref, turned, w_buf, sems = refs
    low = lax.axis_index("lo")
    mine = lax.axis_index("narrow")
    chunks = w_buf.shape[0]
    deep = w_buf.shape[1]
    base = sum(part.shape[0] for part in parts)
    copies = [
        pltpu.make_async_copy(w_ref.at[pl.ds(base + c * deep, deep)], w_buf.at[c], sems.at[c])
        for c in range(chunks)
    ]
    for copy in copies:
        copy.start()
    pair = 2
    rows = 2 * own_ref.shape[0]
    tiles = own_ref.shape[1]
    place_rows(own_ref, turned, pair, 0, lambda j: 2 * j + low)
    place_rows(other_ref, turned, pair, 0, lambda j: 2 * j + (1 - low))
    total = jnp.zeros((rows, w_ref.shape[1]), jnp.float32)
    at = 0
    for part in parts:
        x = turned_rows(turned, rows, tiles, at // LANES, part.shape[0] // LANES)
        total = total + jnp.dot(x, part[...], preferred_element_type=jnp.float32)
        at += part.shape[0]
    for c in range(chunks):
        x = turned_rows(turned, rows, tiles, (at + c * deep) // LANES, deep // LANES)
        copies[c].wait()
        total = total + jnp.dot(x, w_buf[c], preferred_element_type=jnp.float32)
    half = rows // 2
    lower = mine == 0
    keep_ref[...] = jnp.where(lower, total[:half], total[half:])
    send_ref[...] = jnp.where(lower, total[half:], total[:half])


def second_product(own, other, weight, parts):
    rows = 2 * own.shape[0]
    cols = weight.shape[1]
    deep = 512
    chunks = (weight.shape[0] - sum(part.shape[0] for part in parts)) // deep
    weight = pltpu.with_memory_space_constraint(weight, pltpu.HBM)
    parts = [pltpu.with_memory_space_constraint(part, pltpu.VMEM) for part in parts]
    half = jax.ShapeDtypeStruct((rows // 2, cols), jnp.float32)
    return pl.pallas_call(
        second_product_kernel,
        out_shape=(half, half),
        in_specs=[WHOLE, WHOLE, pl.BlockSpec(memory_space=pltpu.HBM)] + [WHOLE] * len(parts),
        out_specs=(WHOLE, WHOLE),
        scratch_shapes=[
            pltpu.VMEM((rows * own.shape[1], LANES), jnp.float32),
            pltpu.VMEM((chunks, deep, cols), weight.dtype),
            pltpu.SemaphoreType.DMA((chunks,)),
        ],
        compiler_params=params(24),
        cost_estimate=pl.CostEstimate(
            flops=2 * rows * weight.size, bytes_accessed=4 * own.size + 2 * weight.size, transcendentals=0
        ),
        name="second_product",
    )(own, other, weight, *parts)


def attention_kernel(
    first,
    length_ref,
    got_ref,
    keys_ref,
    values_ref,
    scale_ref,
    turn_ref,
    w_ref,
    o_ref,
    w_part_ref,
    sem,
):
    ahead = pltpu.make_async_copy(w_ref.at[pl.ds(first, w_part_ref.shape[0])], w_part_ref, sem)
    ahead.start()
    copies, parts, per_part, _ = o_ref.shape
    heads_of = (got_ref.shape[2] - LANES) // LANES
    group = QUERY_HEADS // KEY_VALUE_HEADS
    sources = group // heads_of
    q_cols = heads_of * LANES
    slots = keys_ref.shape[1]
    inverse_scale = HEAD_SIZE ** (-0.5)
    cosine, sine = turn_ref[0:1], turn_ref[1:2]

    def rounded(w, at, size):
        total = got_ref[2 * w, :, at : at + size] + got_ref[2 * w + 1, :, at : at + size]
        return total.astype(jnp.bfloat16).astype(jnp.float32)

    def rotate(x):
        return x * cosine + pltpu.roll(x, HEAD_SIZE // 2, 1) * sine

    live = lax.broadcasted_iota(jnp.int32, (2 * group, slots), 1) < jnp.concatenate(
        [length_ref[...]] * (slots // LANES), axis=1
    )
    none = jnp.zeros((group, HEAD_SIZE), jnp.bfloat16)
    pairs = range(0, KEY_VALUE_HEADS, 2)
    scored = []
    for pair in pairs:
        cache, fresh, fresh_values = [], [], []
        for g in (pair, pair + 1):
            rows = [
                rounded(w, 0, q_cols).reshape(heads_of, LANES)
                for w in range(g * sources, (g + 1) * sources)
            ]
            rotated = rotate(jnp.concatenate(rows, axis=0))
            fresh_key = rotate(rounded(g, q_cols, LANES)).astype(jnp.bfloat16).astype(jnp.float32)
            scale = scale_ref[:, g * HEAD_SIZE : (g + 1) * HEAD_SIZE]
            cache.append((rotated * scale * inverse_scale).astype(jnp.bfloat16))
            fresh_query = (rotated * inverse_scale).astype(jnp.bfloat16).astype(jnp.float32)
            fresh.append(jnp.sum(fresh_query * fresh_key, axis=-1, keepdims=True))
            fresh_values.append(
                jnp.broadcast_to(rounded(KEY_VALUE_HEADS + g, q_cols, LANES), (group, HEAD_SIZE))
            )
        queries = jnp.concatenate(
            [
                jnp.concatenate([cache[0], none], axis=1),
                jnp.concatenate([none, cache[1]], axis=1),
            ],
            axis=0,
        )
        span = slice(pair * HEAD_SIZE, (pair + 2) * HEAD_SIZE)
        scores = lax.dot_general(
            queries,
            keys_ref[0, :, span],
            (((1,), (1,)), ((), ())),
            preferred_element_type=jnp.float32,
        )
        scored.append((scores, jnp.concatenate(fresh, axis=0), fresh_values))
    for pair, (scores, fresh_score, fresh_values) in zip(pairs, scored, strict=True):
        masked = jnp.where(live, scores, jnp.float32(-1e30))
        top = jnp.maximum(jnp.max(masked, axis=-1, keepdims=True), fresh_score)
        exps = jnp.where(live, jnp.exp(masked - top), jnp.float32(0.0))
        fresh_exp = jnp.exp(fresh_score - top)
        total = jnp.sum(exps, axis=-1, keepdims=True) + fresh_exp
        span = slice(pair * HEAD_SIZE, (pair + 2) * HEAD_SIZE)
        both = jnp.dot(
            exps.astype(jnp.bfloat16), values_ref[0, :, span], preferred_element_type=jnp.float32
        )
        summed = jnp.concatenate([both[:group, :HEAD_SIZE], both[group:, HEAD_SIZE:]], axis=0)
        fresh_weight = fresh_exp.astype(jnp.bfloat16).astype(jnp.float32)
        summed = summed + fresh_weight * jnp.concatenate(fresh_values, axis=0)
        attended = (summed / total).astype(jnp.bfloat16)
        part, at = divmod(pair * group, per_part)
        for copy in range(copies):
            o_ref[copy, part, at : at + 2 * group, :] = attended
    ahead.wait()


def attention(
    got, keys, values, scale, lengths, turn, out_weight, first, ahead, copies, parts
):
    out_weight = pltpu.with_memory_space_constraint(out_weight, pltpu.HBM)
    keys = pltpu.with_memory_space_constraint(keys, pltpu.VMEM)
    values = pltpu.with_memory_space_constraint(values, pltpu.VMEM)
    return pl.pallas_call(
        functools.partial(attention_kernel, first),
        out_shape=(
            jax.ShapeDtypeStruct((copies, parts, QUERY_HEADS // parts, HEAD_SIZE), jnp.bfloat16),
            pltpu.VMEM((ahead, out_weight.shape[1]), out_weight.dtype),
        ),
        in_specs=[WHOLE] * 6 + [pl.BlockSpec(memory_space=pltpu.HBM)],
        out_specs=(WHOLE, WHOLE),
        scratch_shapes=[pltpu.SemaphoreType.DMA],
        compiler_params=params(8),
        cost_estimate=pl.CostEstimate(
            flops=4 * QUERY_HEADS * keys.shape[1] * HEAD_SIZE,
            bytes_accessed=4 * keys.size,
            transcendentals=QUERY_HEADS * keys.shape[1],
        ),
        name="attention",
    )(lengths, got, keys, values, scale, turn, out_weight)


def fits(tokens, q_weight, key_value_weight, stored_keys):
    return (
        lax.axis_size(WIDE) == 16
        and lax.axis_size("narrow") == 2
        and tokens.shape[0] == 2
        and stored_keys.shape[0] == 1
        and q_weight.shape[1] % 1024 == 0
        and key_value_weight.shape[1] == LANES
        and q_weight.shape[0] % 8192 == 0
    )


def tiled_body(
    tokens,
    q_weight,
    key_value_weight,
    out_weight,
    stored_keys,
    stored_values,
    channel_key_scale,
    lengths,
):
    count = lax.axis_size(WIDE)
    narrow = lax.axis_size("narrow")
    eighth = q_weight.shape[0] // 8
    q_parts = []
    held, held_rows = tokens, []
    for step, first, last in ((8, 0, 2), (4, 2, 5), (2, 5, 8)):
        other = lax.ppermute(held, WIDE, [(i, i ^ step) for i in range(count)])
        part = load(q_weight, first * eighth, (last - first) * eighth, *held_rows)
        if held_rows:
            held = join(held, other, part)
        else:
            held, turn, lengths = opening(tokens, other, lengths, part)
        q_parts.append(part)
        held_rows = [held]
    other = lax.ppermute(held, WIDE, [(i, i ^ 1) for i in range(count)])
    kv_part = load(key_value_weight, 0, key_value_weight.shape[0], held)
    ahead, next_rows, last_rows = 6144, 512, 512
    partial_terms, first_part = first_product(held, other, q_parts, kv_part, out_weight, ahead)
    got = lax.all_to_all(partial_terms, EVERY, split_axis=0, concat_axis=0, tiled=True)
    attended, next_part = attention(
        got,
        stored_keys,
        stored_values,
        channel_key_scale,
        lengths,
        turn,
        out_weight,
        ahead,
        next_rows,
        lax.axis_size("hi"),
        narrow,
    )
    mine = lax.all_to_all(
        attended.reshape((-1,) + attended.shape[2:]),
        ("hi", "narrow"),
        split_axis=0,
        concat_axis=0,
        tiled=True,
    )
    other = lax.ppermute(mine, "lo", [(0, 1), (1, 0)])
    last_part = load(out_weight, ahead + next_rows, last_rows, mine)
    keep, send = second_product(mine, other, out_weight, (first_part, next_part, last_part))
    return (keep + lax.ppermute(send, "narrow", [(0, 1), (1, 0)])).astype(jnp.bfloat16)


def body(*arguments):
    tokens, q_weight, key_value_weight, _, stored_keys = arguments[:5]
    if fits(tokens, q_weight, key_value_weight, stored_keys):
        return tiled_body(*arguments)
    return general_body(*arguments)


def solution(mesh):
    high, low, narrow = mesh.shape["wide"] // 2, 2, mesh.shape["narrow"]
    fine = Mesh(mesh.devices.reshape(high, low, narrow), EVERY)
    placed = (
        P(WIDE, "narrow"),
        P("narrow", WIDE),
        P("narrow", WIDE),
        P("narrow", WIDE),
        P(EVERY, None, None),
        P(EVERY, None, None),
        P(EVERY, None),
        P(EVERY),
    )
    return jax.shard_map(
        body, mesh=fine, in_specs=placed, out_specs=P("narrow", WIDE), check_vma=False
    )
```
